32 devices in a mesh: wide: 16 (over z, y, core), narrow: 2 (over x).
Axes of the slice: x: 2, y: 2, z: 4, core: 2. Of those that a mesh axis runs over, the one named last changes fastest.
Arguments:
- tokens: bfloat16 [32, 384, 768], P(('wide', 'narrow')), may hold values from -6 to 6
- masked: int32 [32, 384], P(('wide', 'narrow')), may hold values from 0 to 1, as said below
- out_grad: bfloat16 [32, 768, 768], P(('wide', 'narrow')), may hold values from -6 to 6
- slot_block: int32 [16], replicated, may hold values from 0 to 12, as said below
- weights: float32 [16, 768, 768], P('narrow')
- vectors: float32 [6144], P('narrow')
- vec_first: float32 [6144], P('narrow')
- vec_second: float32 [6144], P('narrow'), as said below
- mom_first: float32 [16, 768, 768], P('narrow', 'wide')
- mom_second: float32 [16, 768, 768], P('narrow', 'wide'), as said below
- basis_left: float32 [16, 768, 768], P('narrow', None, 'wide'), as said below
- basis_right: float32 [16, 768, 768], P('narrow'), as said below
Outputs:
- layer_out: bfloat16 [32, 768, 768], P(('wide', 'narrow'))
- in_grad: bfloat16 [32, 384, 768], P(('wide', 'narrow'))
- new_weights: float32 [16, 768, 768], P('narrow')
- new_first: float32 [16, 768, 768], P('narrow', 'wide')
- new_second: float32 [16, 768, 768], P('narrow', 'wide')
- new_vectors: float32 [6144], P('narrow')
- new_vec_first: float32 [6144], P('narrow')
- new_vec_second: float32 [6144], P('narrow')
The draws below stay inside these ranges and needn't reach their ends.
Inputs may be any that keep to these rules, and one draw needn't show every extreme that they name: `slot_block`: each of 0 to 11 appears exactly once; every other entry is 12 and marks a slot that holds no block. `masked`: in each aligned block of 16 positions of a sequence, 5 to 12 entries are 1. `basis_left`: each slot's matrix is orthogonal. `basis_right`: each slot's matrix is orthogonal. `mom_second`: every entry is positive. `vec_second`: every entry is positive.
All inputs are finite; a program needn't handle non-finite values.
Results may differ from the reference program's by a relative error of at most 0.012.
The reference program's roundings to bfloat16 on the way count: a program that leaves them out, or rounds other values in their place, can miss the bound.
Values may be sent and summed in bfloat16 or wider, within the bound.
No kernel may reach another device: no remote copies, remote signals or barrier semaphores. Data moves between devices by JAX's collectives and lax.ppermute only.
A program may use at most 320 MiB of HBM per device.

```python
import math
import jax
import jax.numpy as jnp
from jax import lax

D = 768
HEADS = 12
FF = 3072
BLK = 16
SEQ = 384
SEQS = 32
SLOTS = 16
NBLK = 12
NVEC = 6144
QROWS = 768


def slot_table(key):
    raw_draw = jax.random.randint(jax.random.fold_in(key, 101), (SLOTS,), 0, 1 << 20)
    scores = raw_draw * SLOTS + jnp.arange(SLOTS, dtype=jnp.int32)
    return jnp.minimum(jnp.argsort(scores), NBLK).astype(jnp.int32)


def kind_factor(blocks, factors):
    ff_blocks = FF // D
    return jnp.where(blocks < 2, factors[0], jnp.where(blocks == 2, factors[1], jnp.where(blocks == 3, factors[2], jnp.where(blocks < 4 + ff_blocks, factors[3], jnp.where(blocks < NBLK, factors[4], factors[0]))))).astype(jnp.float32)


def grad_size():
    return math.sqrt(2.0 * SEQ * SEQS)


def moment_factor(key):
    return kind_factor(slot_table(key), (2.0, 2.5, 0.5, 0.6, 1.2)) * grad_size()


def vector_factor():
    pieces = [jnp.full((D,), 1.5), jnp.full((D,), 3.0), jnp.full((D,), 1.0), jnp.full((FF,), 0.6), jnp.full((D,), 1.5)]
    return jnp.concatenate(pieces).astype(jnp.float32) * grad_size()


def spread_draw(key, shape):
    return jnp.exp(jax.random.uniform(key, shape, jnp.float32, 0.0, math.log(4.0)))


def orthogonal(key):
    sub_keys = jax.random.split(key, 3)
    index_row = jnp.arange(D, dtype=jnp.int32)
    row_order = jnp.argsort(jax.random.randint(sub_keys[0], (SLOTS, D), 0, 1 << 20) * D + index_row, axis=1).astype(jnp.int32)
    col_order = jnp.argsort(jax.random.randint(sub_keys[1], (SLOTS, D), 0, 1 << 20) * D + index_row, axis=1).astype(jnp.int32)
    signs = (2 * jax.random.randint(sub_keys[2], (SLOTS, D), 0, 2) - 1).astype(jnp.float32)
    row_part = row_order[:, :, None]
    col_part = col_order[:, None, :]
    phase = (2 * row_part + 1) * col_part % (4 * D)
    cosine = jnp.cos(jnp.pi * phase.astype(jnp.float32) / (2.0 * D))
    norming = jnp.where(col_part == 0, math.sqrt(1.0 / D), math.sqrt(2.0 / D)).astype(jnp.float32)
    return cosine * norming * signs[:, None, :]


def draw_slot_block(key, part):
    return slot_table(key)


def draw_masked(key, part):
    block_count = SEQ // BLK
    counts = jax.random.randint(jax.random.fold_in(key, 111), (SEQS, block_count, 1), 5, 13)
    raw_draw = jax.random.randint(jax.random.fold_in(key, 112), (SEQS, block_count, BLK), 0, 1 << 20)
    scores = raw_draw * BLK + jnp.arange(BLK, dtype=jnp.int32)
    ranks = jnp.argsort(jnp.argsort(scores, axis=-1), axis=-1)
    return (ranks < counts).astype(jnp.int32).reshape(SEQS, SEQ)


def draw_weights(key, part):
    factor = kind_factor(slot_table(key), (D ** (-0.5), D ** (-0.5), 4.0 * D ** (-0.5), D ** (-0.5), FF ** (-0.5)))
    normal_draw = jax.random.normal(jax.random.fold_in(key, 102), (SLOTS, D, D), jnp.float32)
    return normal_draw * factor[:, None, None]


def draw_mom_first(key, part):
    factor = moment_factor(key)
    return jax.random.normal(jax.random.fold_in(key, 103), (SLOTS, D, D), jnp.float32) * factor[:, None, None]


def draw_mom_second(key, part):
    factor = moment_factor(key)
    return spread_draw(jax.random.fold_in(key, 104), (SLOTS, D, D)) * (factor * factor)[:, None, None]


def draw_vectors(key, part):
    sub_keys = jax.random.split(jax.random.fold_in(key, 105), 5)
    pieces = [jax.random.normal(sub_keys[0], (D,), jnp.float32), jax.random.uniform(sub_keys[1], (D,), jnp.float32, 0.5, 1.5), jax.random.uniform(sub_keys[2], (D,), jnp.float32, 0.5, 1.5), 0.5 * jax.random.normal(sub_keys[3], (FF,), jnp.float32), 0.5 * jax.random.normal(sub_keys[4], (D,), jnp.float32)]
    return jnp.concatenate(pieces)


def draw_vec_first(key, part):
    return jax.random.normal(jax.random.fold_in(key, 106), (NVEC,), jnp.float32) * vector_factor()


def draw_vec_second(key, part):
    factor = vector_factor()
    return spread_draw(jax.random.fold_in(key, 107), (NVEC,)) * factor * factor


def draw_basis_left(key, part):
    return orthogonal(jax.random.fold_in(key, 201))


def draw_basis_right(key, part):
    return orthogonal(jax.random.fold_in(key, 202))


def block_levels(rng, extent, shards, smallest, top_value):
    def one(axis_at, parts):
        steps = jax.random.uniform(jax.random.fold_in(jax.random.fold_in(rng, 6), axis_at), (parts,), jnp.float32, smallest / len(shards), top_value / len(shards))
        return jnp.repeat(jnp.exp(steps), extent[axis_at] // parts).reshape((-1,) + (1,) * (len(extent) - axis_at - 1))

    factor_of = one(*shards[0])
    for cut in shards[1:]:
        factor_of = factor_of * one(*cut)
    return factor_of


def noise(stream_key, dims, spread, most, shards=(), kind=jnp.bfloat16):
    values = spread * jax.random.normal(stream_key, dims, jnp.float32)
    if shards:
        values = values * block_levels(stream_key, dims, shards, -0.22, 0.18)
    return jnp.clip(values, -most, most).astype(kind)


def setup_inputs(seed: int = 0) -> dict:
    seeds = jax.random.split(jax.random.key(seed), 13)
    return {
        "tokens": noise(seeds[0], (SEQS, SEQ, D), 1.0, 6.0, ((0, 32),)),
        "masked": draw_masked(jax.random.fold_in(seeds[12], 71), 0),
        "out_grad": noise(seeds[2], (SEQS, 2 * SEQ, D), 1.0, 6.0, ((0, 32),)),
        "slot_block": draw_slot_block(jax.random.fold_in(seeds[12], 71), 0),
        "weights": draw_weights(jax.random.fold_in(seeds[12], 71), 0),
        "vectors": draw_vectors(jax.random.fold_in(seeds[12], 71), 0),
        "vec_first": draw_vec_first(jax.random.fold_in(seeds[12], 71), 0),
        "vec_second": draw_vec_second(jax.random.fold_in(seeds[12], 71), 0),
        "mom_first": draw_mom_first(jax.random.fold_in(seeds[12], 71), 0),
        "mom_second": draw_mom_second(jax.random.fold_in(seeds[12], 71), 0),
        "basis_left": draw_basis_left(jax.random.fold_in(seeds[12], 71), 0),
        "basis_right": draw_basis_right(jax.random.fold_in(seeds[12], 71), 0),
    }


EPS_NORM = 1e-05
EPS_ADAM = 1e-08
RATE_MATRIX = 0.05
RATE_VECTOR = 0.3
BETA = 0.5
MASK_FILL = -1e+30
PRECISE = lax.Precision.HIGHEST

@jax.custom_vjp
def low(v):
    return lax.optimization_barrier(v.astype(jnp.bfloat16)).astype(jnp.float32)

@jax.custom_vjp
def low_back(v):
    return v

def low_keep(v):
    return (low(v), None)

def low_pass(kept, grad):
    return (grad,)

def back_keep(v):
    return (v, None)

def back_low(kept, grad):
    return (low(grad),)
low.defvjp(low_keep, low_pass)
low_back.defvjp(back_keep, back_low)

def product(left, right):
    return jnp.dot(left, right, preferred_element_type=jnp.float32, precision=PRECISE)

def layer_norm(matrix, gain_vec):
    average = lax.optimization_barrier(jnp.mean(matrix, axis=-1, keepdims=True))
    centred = matrix - average
    variance = lax.optimization_barrier(jnp.mean(centred * centred, axis=-1, keepdims=True))
    return centred * lax.rsqrt(variance + EPS_NORM) * gain_vec

def rotary(matrix, direction):
    row_count, row_width = matrix.shape
    half_size = row_width // HEADS // 2
    position = (jnp.arange(row_count, dtype=jnp.int32) % SEQ).astype(jnp.float32)
    frequency = jnp.exp(jnp.arange(half_size, dtype=jnp.float32) * (-2.0 * math.log(10000.0) / (2 * half_size)))
    angles = position[:, None] * frequency[None, :]
    cosine = jnp.cos(angles)[:, None, :]
    sine_term = direction * jnp.sin(angles)[:, None, :]
    pieces = matrix.reshape(row_count, HEADS, 2, half_size)
    lower_half = pieces[:, :, 0]
    upper_half = pieces[:, :, 1]
    turned = jnp.stack([lower_half * cosine - upper_half * sine_term, upper_half * cosine + lower_half * sine_term], axis=2)
    return turned.reshape(row_count, row_width)

def allowed_pairs(row_start, row_count, key_count):
    q_index = row_start + jnp.arange(row_count, dtype=jnp.int32)[:, None]
    k_index = jnp.arange(key_count, dtype=jnp.int32)[None, :]
    q_noisy = q_index < SEQ
    k_noisy = k_index < SEQ
    q_block = q_index % SEQ // BLK
    k_block = k_index % SEQ // BLK
    same_block = q_noisy & k_noisy & (q_block == k_block)
    earlier = q_noisy & ~k_noisy & (k_block < q_block)
    causal = ~q_noisy & ~k_noisy & (k_block <= q_block)
    return same_block | earlier | causal

def attention(queries, key_rows, value_rows):
    row_count = queries.shape[0]
    head_size = D // HEADS
    score_scale = head_size ** (-0.5)
    q_heads = queries.reshape(row_count, HEADS, head_size)
    k_heads = key_rows.reshape(row_count, HEADS, head_size)
    v_heads = value_rows.reshape(row_count, HEADS, head_size)

    def one_block(block_index):
        start = (block_index * QROWS).astype(jnp.int32)
        query_part = lax.dynamic_slice_in_dim(q_heads, start, QROWS, 0)
        raw_scores = low_back(jnp.einsum('qhd,khd->hqk', query_part, k_heads, precision=PRECISE))
        allowed = allowed_pairs(start, QROWS, row_count)
        scores = jnp.where(allowed[None], raw_scores * score_scale, MASK_FILL)
        probs_low = low(jax.nn.softmax(scores, axis=-1))
        return jnp.einsum('hqk,khd->qhd', probs_low, v_heads, precision=PRECISE)
    mixed_all = lax.map(jax.checkpoint(one_block), jnp.arange(row_count // QROWS, dtype=jnp.int32))
    return mixed_all.reshape(row_count, D)

def layer(clean_rows, is_masked, blocks, params):
    ff_blocks = FF // D
    mask_vec = params[0:D]
    gain_one = params[D:2 * D]
    gain_two = params[2 * D:3 * D]
    bias_one = params[3 * D:3 * D + FF]
    bias_two = params[3 * D + FF:]
    noisy_rows = jnp.where(is_masked[:, None] == 1, mask_vec[None, :], clean_rows)
    stacked = jnp.concatenate([noisy_rows, clean_rows], axis=0)
    norm_one = low(layer_norm(stacked, gain_one))
    proj_query = low_back(product(norm_one, blocks[0]))
    proj_key = low_back(product(norm_one, blocks[1]))
    proj_value = low_back(product(norm_one, blocks[2]))
    queries = low(rotary(proj_query, 1.0))
    key_rows = low(rotary(proj_key, 1.0))
    value_rows = low(proj_value)
    mixed_rows = low(low_back(attention(queries, key_rows, value_rows)))
    resid = stacked + low_back(product(mixed_rows, blocks[3]))
    norm_two = low(layer_norm(resid, gain_two))
    up_matrix = jnp.concatenate([blocks[4 + f] for f in range(ff_blocks)], axis=1)
    hidden = low_back(product(norm_two, up_matrix)) + bias_one
    active = low(jax.nn.gelu(hidden, approximate=True))
    down_matrix = blocks[4 + ff_blocks:].reshape(FF, D)
    return resid + low_back(product(active, down_matrix)) + bias_two

def reference(tokens, masked, out_grad, slot_block, weights, vectors, vec_first, vec_second, mom_first, mom_second, basis_left, basis_right):
    block_slot = jnp.argmax((slot_block[None, :] == jnp.arange(NBLK, dtype=jnp.int32)[:, None]).astype(jnp.int32), axis=1).astype(jnp.int32)

    def total(clean_all, weight_all, vector_all):
        blocks = low(weight_all)[block_slot]
        params = low(vector_all)

        def one_seq(pair):
            return layer(pair[0], pair[1], blocks, params)
        return lax.map(jax.checkpoint(one_seq), (clean_all, masked))
    result, pullback = jax.vjp(total, tokens.astype(jnp.float32), weights, vectors)
    grad_tokens, grad_weights, grad_vectors = pullback(out_grad.astype(jnp.float32))
    layer_out = result.astype(jnp.bfloat16)
    in_grad = grad_tokens.astype(jnp.bfloat16)
    half_turn = jnp.einsum('sdi,sdk->sik', basis_left, grad_weights, precision=PRECISE)
    rotated = jnp.einsum('sik,skj->sij', half_turn, basis_right, precision=PRECISE)
    first_new = BETA * mom_first + (1.0 - BETA) * rotated
    second_new = BETA * mom_second + (1.0 - BETA) * rotated * rotated
    step_rot = first_new / (jnp.sqrt(second_new) + EPS_ADAM)
    back_half = jnp.einsum('sik,sjk->sij', step_rot, basis_right, precision=PRECISE)
    step_full = jnp.einsum('sdi,sij->sdj', basis_left, back_half, precision=PRECISE)
    live_flag = (slot_block < NBLK)[:, None, None]
    new_weights = jnp.where(live_flag, weights - RATE_MATRIX * step_full, 0.0)
    new_first = jnp.where(live_flag, first_new, 0.0)
    new_second = jnp.where(live_flag, second_new, 0.0)
    vec_mean = BETA * vec_first + (1.0 - BETA) * grad_vectors
    vec_square = BETA * vec_second + (1.0 - BETA) * grad_vectors * grad_vectors
    vec_new = vectors - RATE_VECTOR * vec_mean / (jnp.sqrt(vec_square) + EPS_ADAM)
    return (layer_out, in_grad, new_weights, new_first, new_second, vec_new, vec_mean, vec_square)
```

```python
from functools import partial
import math

import jax
import jax.numpy as jnp
from jax import lax
from jax.experimental import pallas as pl
from jax.experimental.pallas import tpu as pltpu
from jax.sharding import PartitionSpec as P

D = 768
HEADS = 12
FF = 3072
BLK = 16
SEQ = 384
NBLK = 12
ROWS = 2 * SEQ
FFB = FF // D
PAIR = 128
NPAIR = D // PAIR
TILE = 128
CHUNK = 256

EPS_NORM = 1e-05
EPS_ADAM = 1e-08
RATE_MATRIX = 0.05
RATE_VECTOR = 0.3
BETA = 0.5
MASK_FILL = -1e30
GELU_A = math.sqrt(2.0 / math.pi)
GELU_B = 0.044715

BF = jnp.bfloat16
F32 = jnp.float32


NT = (((1,), (1,)), ((), ()))
TN = (((0,), (0,)), ((), ()))
NN = (((1,), (0,)), ((), ()))


def mm(a, b, dims=NN):
    return lax.dot_general(a, b, dims, preferred_element_type=F32)


def any_spec():
    return pl.BlockSpec(memory_space=pl.ANY)


def xor_permute(x, axis, size, mask):
    return lax.ppermute(x, axis, [(i, i ^ mask) for i in range(size)])


def tree_gather(x, axis, size, order):
    have = {0: x}
    for bit in order:
        fresh = {r | bit: xor_permute(have[r], axis, size, bit) for r in have}
        have.update(fresh)
    return [have[r] for r in range(size)]


def far_first(size):
    bits = []
    bit = size // 2
    while bit:
        bits.append(bit)
        bit //= 2
    return bits


def tree_scatter(keep, send, axis, size, order):
    parts = [keep, xor_permute(send, axis, size, order[0])]
    cur = size // 2
    for bit in order[1:]:
        half = cur // 2
        total = parts[0][half:cur].astype(F32)
        for p in parts[1:]:
            total = total + p[half:cur].astype(F32)
        got = xor_permute(total.astype(BF), axis, size, bit)
        parts = [p[:half] for p in parts] + [got]
        cur = half
    total = parts[0][0].astype(F32)
    for p in parts[1:]:
        total = total + p[0].astype(F32)
    return total


def butterfly_sum(x, axis, size, order, low=None):
    for bit in order:
        sent = x if low is None else x.astype(low)
        x = x + xor_permute(sent, axis, size, bit).astype(x.dtype)
    return x


def position(r, order):
    pos = 0
    for bit in order:
        pos = pos * 2 + (1 if r & bit else 0)
    return pos


def start_slices(refs, index, dst, sem, me):
    rows = D // len(refs)
    for r, ref in enumerate(refs):
        at = pl.multiple_of((me ^ r) * rows, rows)
        pltpu.make_async_copy(ref.at[index], dst.at[pl.ds(at, rows)], sem).start()


def start_block(meta, block, own, first, second, dst, sem):
    me = meta[0]
    source = meta[1 + block]
    index = meta[1 + NBLK + block]

    @pl.when(source == 0)
    def _():
        pltpu.make_async_copy(own.at[index], dst, sem).start()

    @pl.when(source == 1)
    def _():
        start_slices(first, index, dst, sem, me)

    if second:

        @pl.when(source == 2)
        def _():
            start_slices(second, index, dst, sem, me)


def wait_block(dst, sem):
    pltpu.make_async_copy(dst, dst, sem).wait()


def norm_stats(z):
    mean = jnp.mean(z, axis=-1, keepdims=True)
    cen = z - mean
    var = jnp.mean(cen * cen, axis=-1, keepdims=True)
    return cen, lax.rsqrt(var + EPS_NORM)


def norm_back(zh, r, dz):
    return r * (
        dz
        - jnp.mean(dz, axis=-1, keepdims=True)
        - zh * jnp.mean(dz * zh, axis=-1, keepdims=True)
    )


def half_swap(z):
    lane = lax.broadcasted_iota(jnp.int32, z.shape, 1) % 64
    return jnp.where(lane < 32, pltpu.roll(z, PAIR - 32, 1), pltpu.roll(z, 32, 1))


def tile_masks():
    key = lax.broadcasted_iota(jnp.int32, (TILE, 2 * TILE), 0) // BLK
    qry = lax.broadcasted_iota(jnp.int32, (TILE, 2 * TILE), 1) % TILE // BLK
    return key == qry, key < qry, key <= qry


def head_split(x):
    lane = lax.broadcasted_iota(jnp.int32, x.shape, 1)
    zero = jnp.zeros_like(x)
    return jnp.concatenate([jnp.where(lane < 64, x, zero), jnp.where(lane < 64, zero, x)], axis=0)


def head_join(xt):
    row = lax.broadcasted_iota(jnp.int32, (PAIR, TILE), 0)
    return jnp.where(row < 64, xt[:, :TILE], xt[:, TILE:])


def key_parts(noised, t, masks):
    same, before, upto = masks
    parts = []
    if t > 0:
        parts.append((SEQ, TILE * t, None))
    parts.append((SEQ + TILE * t, TILE, before if noised else upto))
    if noised:
        parts.append((TILE * t, TILE, same))
    return parts


def masked_scores(k_ref, lanes, parts, qs):
    out = []
    for start, count, mask in parts:
        s = mm(k_ref[pl.ds(start, count), lanes], qs, NT)
        out.append(s if mask is None else jnp.where(mask, s, MASK_FILL))
    return out


def total_of(items):
    total = items[0]
    for x in items[1:]:
        total = total + x
    return total


def input_rows(tok_ref, mask_ref, vp_ref, half):
    tok = tok_ref[...].astype(F32)
    if half == 1:
        return tok
    return jnp.where(mask_ref[...] == 1, vp_ref[0:1, :], tok)


def forward_kernel(nw, meta, tok, maskc, vp, cos, sin, own, *refs):
    first = refs[:nw]
    q_ref, k_ref, v_ref, n1_ref, o_ref, lse_ref, x2_ref, n2_ref = refs[nw : nw + 8]
    wbuf, sems = refs[nw + 8 :]
    for b in range(4):
        start_block(meta, b, own, first, (), wbuf.at[b], sems.at[b])
    for half in range(2):
        cen, r = norm_stats(input_rows(tok, maskc, vp, half))
        n1_ref[half * SEQ : (half + 1) * SEQ, :] = (cen * r * vp[1:2, :]).astype(BF)
    for b, out in enumerate((q_ref, k_ref, v_ref)):
        wait_block(wbuf.at[b], sems.at[b])
        for half in range(2):
            rows = slice(half * SEQ, (half + 1) * SEQ)
            for c in range(D // CHUNK):
                z = mm(n1_ref[rows, :], wbuf[b, :, c * CHUNK : (c + 1) * CHUNK])
                for s in range(CHUNK // PAIR):
                    piece = z[:, s * PAIR : (s + 1) * PAIR]
                    if b < 2:
                        piece = piece * cos[...] + half_swap(piece) * sin[...]
                    if b == 0:
                        piece = piece * 0.125
                    at = c * CHUNK + s * PAIR
                    out[rows, at : at + PAIR] = piece.astype(BF)

    masks = tile_masks()

    def one_pair(p, carry):
        lanes = pl.ds(pl.multiple_of(p * PAIR, PAIR), PAIR)
        for noised in (True, False):
            for t in range(SEQ // TILE):
                row = (0 if noised else SEQ) + TILE * t
                qs = head_split(q_ref[pl.ds(row, TILE), lanes])
                parts = key_parts(noised, t, masks)
                scores = masked_scores(k_ref, lanes, parts, qs)
                tops = [jnp.max(s, axis=0, keepdims=True) for s in scores]
                top = tops[0]
                for x in tops[1:]:
                    top = jnp.maximum(top, x)
                expo = [jnp.exp(s - top) for s in scores]
                total = total_of([jnp.sum(e, axis=0, keepdims=True) for e in expo])
                mixed = total_of(
                    [
                        mm(v_ref[pl.ds(start, count), lanes], e.astype(BF), TN)
                        for (start, count, _), e in zip(parts, expo)
                    ]
                )
                mixed = mixed * (1.0 / total)
                o_ref[pl.ds(row, TILE), lanes] = head_join(mixed).T.astype(BF)
                lse = top + jnp.log(total)
                lse_ref[p, 0:1, row : row + TILE] = lse[:, :TILE]
                lse_ref[p, 1:2, row : row + TILE] = lse[:, TILE:]
        return carry

    lax.fori_loop(0, NPAIR, one_pair, 0)
    wait_block(wbuf.at[3], sems.at[3])
    for half in range(2):
        rows = slice(half * SEQ, (half + 1) * SEQ)
        x2 = input_rows(tok, maskc, vp, half) + mm(o_ref[rows, :], wbuf[3])
        x2_ref[rows, :] = x2
        cen, r = norm_stats(x2)
        n2_ref[rows, :] = (cen * r * vp[2:3, :]).astype(BF)


def run_forward(meta, tok, maskc, vp, cos, sin, own, first):
    vm = pl.BlockSpec(memory_space=pltpu.VMEM)
    sq = jax.ShapeDtypeStruct((ROWS, D), BF)
    return pl.pallas_call(
        partial(forward_kernel, len(first)),
        name="forward_attention",
        out_shape=(
            sq,
            sq,
            sq,
            sq,
            sq,
            jax.ShapeDtypeStruct((NPAIR, 2, ROWS), F32),
            jax.ShapeDtypeStruct((ROWS, D), F32),
            sq,
        ),
        in_specs=[pl.BlockSpec(memory_space=pltpu.SMEM)] + [vm] * 5 + [any_spec()] * (1 + len(first)),
        out_specs=(vm,) * 8,
        scratch_shapes=[pltpu.VMEM((4, D, D), BF), pltpu.SemaphoreType.DMA((4,))],
    )(meta, tok, maskc, vp, cos, sin, own, *first)


def ffn_kernel(nw, ns, meta, n2, og, x2, vp, own, *refs):
    first = refs[:nw]
    second = refs[nw : nw + ns]
    layer_ref, gup_ref, gdown_ref, dn2_ref, gbias_ref = refs[nw + ns : nw + ns + 5]
    wup, wdown, yacc, act, dhid, sems = refs[nw + ns + 5 :]
    f = pl.program_id(0)

    @pl.when(f == 0)
    def _():
        for b in range(FFB):
            start_block(meta, 4 + b, own, first, second, wup.at[b], sems.at[b])
            start_block(meta, 8 + b, own, first, second, wdown.at[b], sems.at[4 + b])
        yacc[...] = jnp.zeros_like(yacc)
        dn2_ref[...] = jnp.zeros_like(dn2_ref)
        gbias_ref[FFB : FFB + 1, :] = jnp.sum(og[...].astype(F32), axis=0, keepdims=True)

    wait_block(wup.at[f], sems.at[f])
    wait_block(wdown.at[f], sems.at[4 + f])
    bias = vp[pl.ds(3 + f, 1), :]
    gb = jnp.zeros((1, D), F32)
    for c in range(ROWS // CHUNK):
        rows = slice(c * CHUNK, (c + 1) * CHUNK)
        h = mm(n2[rows, :], wup[f]) + bias
        hh = h * h
        th = jnp.tanh(h * (GELU_A + (GELU_A * GELU_B) * hh))
        lift = 0.5 + 0.5 * th
        slope = lift + (0.5 * h) * (1.0 - th * th) * (GELU_A + (3.0 * GELU_A * GELU_B) * hh)
        act[rows, :] = (h * lift).astype(BF)
        dh = mm(og[rows, :], wdown[f], NT) * slope
        gb = gb + jnp.sum(dh, axis=0, keepdims=True)
        dhid[rows, :] = dh.astype(BF)
        yacc[rows, :] += mm(act[rows, :], wdown[f])
        dn2_ref[rows, :] += mm(dhid[rows, :], wup[f], NT)
    gbias_ref[pl.ds(f, 1), :] = gb
    gdown_ref[0] = mm(act[...], og[...], TN).astype(BF)
    gup_ref[0] = mm(n2[...], dhid[...], TN).astype(BF)

    @pl.when(f == FFB - 1)
    def _():
        layer_ref[...] = (x2[...] + yacc[...] + vp[7:8, :]).astype(BF)


def run_ffn(meta, n2, og, x2, vp, own, first, second):
    def whole(shape):
        return pl.BlockSpec(shape, lambda f: (0,) * len(shape))

    grads = pl.BlockSpec((1, D, D), lambda f: (f, 0, 0))
    return pl.pallas_call(
        partial(ffn_kernel, len(first), len(second)),
        name="feed_forward",
        grid=(FFB,),
        out_shape=(
            jax.ShapeDtypeStruct((ROWS, D), BF),
            jax.ShapeDtypeStruct((FFB, D, D), BF),
            jax.ShapeDtypeStruct((FFB, D, D), BF),
            jax.ShapeDtypeStruct((ROWS, D), F32),
            jax.ShapeDtypeStruct((8, D), F32),
        ),
        in_specs=[
            pl.BlockSpec(memory_space=pltpu.SMEM),
            whole((ROWS, D)),
            whole((ROWS, D)),
            whole((ROWS, D)),
            whole((8, D)),
        ]
        + [any_spec()] * (1 + len(first) + len(second)),
        out_specs=(whole((ROWS, D)), grads, grads, whole((ROWS, D)), whole((8, D))),
        scratch_shapes=[
            pltpu.VMEM((FFB, D, D), BF),
            pltpu.VMEM((FFB, D, D), BF),
            pltpu.VMEM((ROWS, D), F32),
            pltpu.VMEM((ROWS, D), BF),
            pltpu.VMEM((ROWS, D), BF),
            pltpu.SemaphoreType.DMA((2 * FFB,)),
        ],
    )(meta, n2, og, x2, vp, own, *first, *second)


def resid_kernel(nw, meta, x2, dn2, og, vp, o_ref, own, *refs):
    first = refs[:nw]
    dx2_ref, do_ref, gwo_ref, gg_ref = refs[nw : nw + 4]
    wbuf, dlow, sems = refs[nw + 4 :]
    start_block(meta, 3, own, first, (), wbuf, sems.at[0])
    gg = jnp.zeros((1, D), F32)
    for c in range(ROWS // CHUNK):
        rows = slice(c * CHUNK, (c + 1) * CHUNK)
        cen, r = norm_stats(x2[rows, :])
        zh = cen * r
        dn = dn2[rows, :]
        gg = gg + jnp.sum(dn * zh, axis=0, keepdims=True)
        dx = og[rows, :].astype(F32) + norm_back(zh, r, dn * vp[2:3, :])
        dx2_ref[rows, :] = dx
        dlow[rows, :] = dx.astype(BF)
    gg_ref[...] = gg
    gwo_ref[0] = mm(o_ref[...], dlow[...], TN).astype(BF)
    wait_block(wbuf, sems.at[0])
    do_ref[...] = mm(dlow[...], wbuf[...], NT).astype(BF)


def run_resid(meta, x2, dn2, og, vp, mixed, own, first):
    vm = pl.BlockSpec(memory_space=pltpu.VMEM)
    return pl.pallas_call(
        partial(resid_kernel, len(first)),
        name="residual_back",
        out_shape=(
            jax.ShapeDtypeStruct((ROWS, D), F32),
            jax.ShapeDtypeStruct((ROWS, D), BF),
            jax.ShapeDtypeStruct((1, D, D), BF),
            jax.ShapeDtypeStruct((1, D), F32),
        ),
        in_specs=[pl.BlockSpec(memory_space=pltpu.SMEM)] + [vm] * 5 + [any_spec()] * (1 + len(first)),
        out_specs=(vm,) * 4,
        scratch_shapes=[
            pltpu.VMEM((D, D), BF),
            pltpu.VMEM((ROWS, D), BF),
            pltpu.SemaphoreType.DMA((1,)),
        ],
    )(meta, x2, dn2, og, vp, mixed, own, *first)


def attention_back_kernel(q, k, v, do, lse_ref, cos, sin, pq, pk, pv, dk, dv):
    masks = tile_masks()

    def one_pair(p, carry):
        lanes = pl.ds(pl.multiple_of(p * PAIR, PAIR), PAIR)
        dk[...] = jnp.zeros_like(dk)
        dv[...] = jnp.zeros_like(dv)
        for noised in (True, False):
            for t in range(SEQ // TILE):
                row = (0 if noised else SEQ) + TILE * t
                qs = head_split(q[pl.ds(row, TILE), lanes])
                ds = head_split(do[pl.ds(row, TILE), lanes])
                lse = jnp.concatenate(
                    [lse_ref[p, 0:1, row : row + TILE], lse_ref[p, 1:2, row : row + TILE]], axis=1
                )
                parts = key_parts(noised, t, masks)
                probs = [jnp.exp(s - lse) for s in masked_scores(k, lanes, parts, qs)]
                prods = []
                for (start, count, _), e in zip(parts, probs):
                    prods.append(e * mm(v[pl.ds(start, count), lanes], ds, NT))
                    dv[start : start + count, :] += mm(e.astype(BF), ds)
                dot = total_of([jnp.sum(x, axis=0, keepdims=True) for x in prods])
                dq = None
                for (start, count, _), e, x in zip(parts, probs, prods):
                    g = (x - e * dot).astype(BF)
                    dk[start : start + count, :] += mm(g, qs)
                    one = mm(k[pl.ds(start, count), lanes], g, TN)
                    dq = one if dq is None else dq + one
                dq = head_join(dq).T * 0.125
                at = TILE * t
                turn = dq * cos[at : at + TILE, :] - half_swap(dq) * sin[at : at + TILE, :]
                pq[pl.ds(row, TILE), lanes] = turn.astype(BF)
        for half in range(2):
            rows = slice(half * SEQ, (half + 1) * SEQ)
            z = dk[rows, :]
            pk[rows, lanes] = (z * cos[...] - half_swap(z) * sin[...]).astype(BF)
            pv[rows, lanes] = dv[rows, :].astype(BF)
        return carry

    lax.fori_loop(0, NPAIR, one_pair, 0)


def run_attention_back(q, k, v, do, lse, cos, sin):
    vm = pl.BlockSpec(memory_space=pltpu.VMEM)
    sq = jax.ShapeDtypeStruct((ROWS, D), BF)
    return pl.pallas_call(
        attention_back_kernel,
        name="attention_back",
        out_shape=(sq, sq, sq),
        in_specs=[vm] * 7,
        out_specs=(vm,) * 3,
        scratch_shapes=[pltpu.VMEM((ROWS, PAIR), F32), pltpu.VMEM((ROWS, PAIR), F32)],
    )(q, k, v, do, lse, cos, sin)


def qkv_grad_kernel(n1, pq, pk, pv, out):
    for i, x in enumerate((pq, pk, pv)):
        out[i] = mm(n1[...], x[...], TN).astype(BF)


def run_qkv_grad(n1, pq, pk, pv):
    vm = pl.BlockSpec(memory_space=pltpu.VMEM)
    return pl.pallas_call(
        qkv_grad_kernel,
        name="qkv_grad",
        out_shape=jax.ShapeDtypeStruct((3, D, D), BF),
        in_specs=[vm] * 4,
        out_specs=vm,
    )(n1, pq, pk, pv)


def input_grad_kernel(nw, meta, tok, maskc, vp, dx2, pq, pk, pv, own, *refs):
    first = refs[:nw]
    in_ref, ge_ref, gg_ref = refs[nw : nw + 3]
    wbuf, sems = refs[nw + 3 :]
    for b in range(3):
        start_block(meta, b, own, first, (), wbuf.at[b], sems.at[b])
    for b in range(3):
        wait_block(wbuf.at[b], sems.at[b])
    gg = jnp.zeros((1, D), F32)
    kept = None
    for half in range(2):
        rows = slice(half * SEQ, (half + 1) * SEQ)
        dn = total_of([mm(x[rows, :], wbuf[b], NT) for b, x in enumerate((pq, pk, pv))])
        cen, r = norm_stats(input_rows(tok, maskc, vp, half))
        zh = cen * r
        gg = gg + jnp.sum(dn * zh, axis=0, keepdims=True)
        dx = dx2[rows, :] + norm_back(zh, r, dn * vp[1:2, :])
        if half == 0:
            hit = maskc[...] == 1
            ge_ref[...] = jnp.sum(jnp.where(hit, dx, 0.0), axis=0, keepdims=True)
            kept = jnp.where(hit, 0.0, dx)
        else:
            in_ref[...] = (dx + kept).astype(BF)
    gg_ref[...] = gg


def run_input_grad(meta, tok, maskc, vp, dx2, pq, pk, pv, own, first):
    vm = pl.BlockSpec(memory_space=pltpu.VMEM)
    return pl.pallas_call(
        partial(input_grad_kernel, len(first)),
        name="input_grad",
        out_shape=(
            jax.ShapeDtypeStruct((SEQ, D), BF),
            jax.ShapeDtypeStruct((1, D), F32),
            jax.ShapeDtypeStruct((1, D), F32),
        ),
        in_specs=[pl.BlockSpec(memory_space=pltpu.SMEM)] + [vm] * 7 + [any_spec()] * (1 + len(first)),
        out_specs=(vm,) * 3,
        scratch_shapes=[pltpu.VMEM((3, D, D), BF), pltpu.SemaphoreType.DMA((3,))],
    )(meta, tok, maskc, vp, dx2, pq, pk, pv, own, *first)


def turn_kernel(nw, offset, order, meta, grad, *refs):
    bases = refs[:nw]
    keep, send = refs[nw : nw + 2]
    lbuf, res, lsem, osem = refs[nw + 2 :]
    b = pl.program_id(0)
    nb = pl.num_programs(0)
    me = meta[0]
    rows = D // nw
    slot = b % 2

    @pl.when(b == 0)
    def _():
        start_slices(bases, offset, lbuf.at[0], lsem.at[0], me)

    @pl.when(b + 1 < nb)
    def _():
        start_slices(bases, offset + b + 1, lbuf.at[1 - slot], lsem.at[1 - slot], me)

    wait_block(lbuf.at[slot], lsem.at[slot])

    @pl.when(b > 1)
    def _():
        wait_block(res.at[slot], osem.at[slot])

    res[slot] = mm(lbuf[slot], grad[0]).astype(BF)
    for r in range(nw):
        pos = position(r, order)
        dst = keep if pos < nw // 2 else send
        at = pl.multiple_of((me ^ r) * rows, rows)
        pltpu.make_async_copy(
            res.at[slot, pl.ds(at, rows)], dst.at[pos % (nw // 2), b], osem.at[slot]
        ).start()

    @pl.when(b == nb - 1)
    def _():
        wait_block(res.at[slot], osem.at[slot])

        @pl.when(b > 0)
        def _():
            wait_block(res.at[1 - slot], osem.at[1 - slot])


def run_turn(meta, grad, bases, offset, order):
    nw = len(bases)
    nb = grad.shape[0]
    out = jax.ShapeDtypeStruct((nw // 2, nb, D // nw, D), BF)
    return pl.pallas_call(
        partial(turn_kernel, nw, offset, order),
        name="gradient_turn",
        grid=(nb,),
        out_shape=(out, out),
        in_specs=[
            pl.BlockSpec(memory_space=pltpu.SMEM),
            pl.BlockSpec((1, D, D), lambda b: (b, 0, 0)),
        ]
        + [any_spec()] * nw,
        out_specs=(any_spec(), any_spec()),
        scratch_shapes=[
            pltpu.VMEM((2, D, D), BF),
            pltpu.VMEM((2, D, D), BF),
            pltpu.SemaphoreType.DMA((2,)),
            pltpu.SemaphoreType.DMA((2,)),
        ],
    )(meta, grad, *bases)


def adam_kernel(blocks, grads, first, second, right, nf, ns, back):
    s = pl.program_id(0)
    live = blocks[s] < NBLK

    @pl.when(live)
    def _():
        basis = right[0].astype(BF)
        turned = mm(grads[0].astype(BF), basis)
        one = BETA * first[0] + (1.0 - BETA) * turned
        two = BETA * second[0] + (1.0 - BETA) * turned * turned
        nf[0] = one
        ns[0] = two
        step = one / (jnp.sqrt(two) + EPS_ADAM)
        back[0] = mm(step.astype(BF), basis, NT).astype(BF)

    @pl.when(jnp.logical_not(live))
    def _():
        nf[...] = jnp.zeros_like(nf)
        ns[...] = jnp.zeros_like(ns)
        back[...] = jnp.zeros_like(back)


def run_adam(blocks, grads, first, second, right):
    count, rows, _ = first.shape
    state = pl.BlockSpec((1, rows, D), lambda s, blocks: (s, 0, 0))
    return pl.pallas_call(
        adam_kernel,
        name="adam_step",
        grid_spec=pltpu.PrefetchScalarGridSpec(
            num_scalar_prefetch=1,
            grid=(count,),
            in_specs=[
                pl.BlockSpec(
                    (1, rows, D), lambda s, blocks: (jnp.minimum(blocks[s], NBLK - 1), 0, 0)
                ),
                state,
                state,
                pl.BlockSpec((1, D, D), lambda s, blocks: (s, 0, 0)),
            ],
            out_specs=(state, state, state),
        ),
        out_shape=(
            jax.ShapeDtypeStruct(first.shape, F32),
            jax.ShapeDtypeStruct(first.shape, F32),
            jax.ShapeDtypeStruct(first.shape, BF),
        ),
    )(blocks, grads, first, second, right)


def update_kernel(nw, blocks, meta, weights, *refs):
    backs = refs[:nw]
    low = refs[nw : 2 * nw]
    high = refs[2 * nw : 3 * nw]
    out = refs[3 * nw]
    lbuf, bbuf, lsem, bsem = refs[3 * nw + 1 :]
    s = pl.program_id(0)
    count = pl.num_programs(0)
    me = meta[0]
    slot = s % 2

    def begin(item, where):
        block = blocks[item]

        @pl.when(block < NBLK)
        def _():
            start_slices(backs, item, bbuf.at[where], bsem.at[where], me)

        @pl.when(block < 4)
        def _():
            start_slices(low, block, lbuf.at[where], lsem.at[where], me)

        @pl.when(jnp.logical_and(block >= 4, block < NBLK))
        def _():
            start_slices(high, block - 4, lbuf.at[where], lsem.at[where], me)

    @pl.when(s == 0)
    def _():
        begin(0, 0)

    @pl.when(s + 1 < count)
    def _():
        begin(s + 1, 1 - slot)

    live = blocks[s] < NBLK

    @pl.when(live)
    def _():
        wait_block(lbuf.at[slot], lsem.at[slot])
        wait_block(bbuf.at[slot], bsem.at[slot])
        out[0] = weights[0] - RATE_MATRIX * mm(lbuf[slot], bbuf[slot], TN)

    @pl.when(jnp.logical_not(live))
    def _():
        out[...] = jnp.zeros_like(out)


def run_update(blocks, meta, weights, backs, low, high):
    nw = len(backs)
    whole = pl.BlockSpec((1, D, D), lambda s, *_: (s, 0, 0))
    return pl.pallas_call(
        partial(update_kernel, nw),
        name="weight_update",
        grid_spec=pltpu.PrefetchScalarGridSpec(
            num_scalar_prefetch=2,
            grid=(weights.shape[0],),
            in_specs=[whole] + [any_spec()] * (3 * nw),
            out_specs=whole,
            scratch_shapes=[
                pltpu.VMEM((2, D, D), BF),
                pltpu.VMEM((2, D, D), BF),
                pltpu.SemaphoreType.DMA((2,)),
                pltpu.SemaphoreType.DMA((2,)),
            ],
        ),
        out_shape=jax.ShapeDtypeStruct(weights.shape, F32),
    )(blocks, meta, weights, *backs, *low, *high)


def rotary_tables():
    half_size = D // HEADS // 2
    position_col = jnp.arange(SEQ, dtype=jnp.int32).astype(F32)
    frequency = jnp.exp(
        jnp.arange(half_size, dtype=F32) * (-2.0 * math.log(10000.0) / (2 * half_size))
    )
    angles = position_col[:, None] * frequency[None, :]
    cosine = jnp.cos(angles)
    sine = jnp.sin(angles)
    return (
        jnp.concatenate([cosine, cosine, cosine, cosine], axis=1),
        jnp.concatenate([-sine, sine, -sine, sine], axis=1),
    )


def on_device(
    nwide,
    nnarrow,
    tokens,
    masked,
    out_grad,
    slot_block,
    weights,
    vectors,
    vec_first,
    vec_second,
    mom_first,
    mom_second,
    basis_left,
    basis_right,
):
    sd = weights.shape[0]
    slots = sd * nnarrow
    rows = D // nwide
    w = lax.axis_index("wide").astype(jnp.int32)
    n = lax.axis_index("narrow").astype(jnp.int32)
    wide_order = far_first(nwide)
    near_order = wide_order[::-1]
    narrow_order = far_first(nnarrow)

    ids = jnp.arange(slots, dtype=jnp.int32)
    live = slot_block < NBLK
    hits = slot_block[None, :] == jnp.arange(NBLK, dtype=jnp.int32)[:, None]
    block_slot = jnp.sum(jnp.where(hits, ids[None, :], 0), axis=1)
    earlier = (
        (slot_block[None, :] < slot_block[:, None])
        | ((slot_block[None, :] == slot_block[:, None]) & (ids[None, :] < ids[:, None]))
    ) & (ids[None, :] // sd == ids[:, None] // sd)
    slot_rank = jnp.sum(earlier.astype(jnp.int32), axis=1)
    block_rank = jnp.sum(jnp.where(hits, slot_rank[None, :], 0), axis=1)
    far = n ^ (block_slot // sd)
    c1 = min(4, sd)
    c2 = sd - c1
    source = jnp.where(far == 0, 0, jnp.where(block_rank < c1, 1, 2))
    index = jnp.where(
        far == 0,
        block_slot % sd,
        jnp.where(
            block_rank < c1, (far - 1) * c1 + block_rank, (far - 1) * c2 + block_rank - c1
        ),
    )
    meta = jnp.concatenate([w[None], source, index]).astype(jnp.int32)
    own_blocks = lax.dynamic_slice_in_dim(slot_block, n * sd, sd)
    own_rank = lax.dynamic_slice_in_dim(slot_rank, n * sd, sd)
    sorted_slots = jnp.sum(
        jnp.where(
            own_rank[None, :] == jnp.arange(sd, dtype=jnp.int32)[:, None],
            jnp.arange(sd, dtype=jnp.int32)[None, :],
            0,
        ),
        axis=1,
    )

    mine = lax.dynamic_slice_in_dim(weights, w * rows, rows, axis=1).astype(BF)[sorted_slots]
    first_x = tree_gather(mine[:c1], "narrow", nnarrow, narrow_order)[1:]
    first = tree_gather(
        jnp.concatenate(first_x, axis=0) if len(first_x) > 1 else first_x[0],
        "wide",
        nwide,
        wide_order,
    )
    second = []
    if c2:
        second_x = tree_gather(mine[c1:], "narrow", nnarrow, narrow_order)[1:]
        second = tree_gather(
            jnp.concatenate(second_x, axis=0) if len(second_x) > 1 else second_x[0],
            "wide",
            nwide,
            wide_order,
        )
    own = weights.astype(BF)

    vec_parts = tree_gather(vectors.astype(BF), "narrow", nnarrow, narrow_order)
    vec_rel = jnp.stack(vec_parts)
    vec_all = vec_rel[n ^ jnp.arange(nnarrow, dtype=jnp.int32)].reshape(8, D).astype(F32)

    left = basis_left.transpose(0, 2, 1).astype(BF)
    left_x = tree_gather(left, "narrow", nnarrow, narrow_order)
    left_all = jnp.concatenate(left_x, axis=0)[far * sd + block_slot % sd]
    left_low = tree_gather(left_all[:4], "wide", nwide, wide_order)
    left_high = tree_gather(left_all[4:], "wide", nwide, wide_order)

    cos, sin = rotary_tables()
    tok = tokens[0]
    maskc = masked[0][:, None]
    og = out_grad[0]

    q, k, v, n1, mixed, lse, x2, n2 = run_forward(meta, tok, maskc, vec_all, cos, sin, own, first)
    layer_out, gup, gdown, dn2, gbias = run_ffn(meta, n2, og, x2, vec_all, own, first, second)

    def reduced(grad, bases, offset):
        keep, send = run_turn(meta, grad, bases, offset, near_order)
        mine_sum = tree_scatter(keep, send, "wide", nwide, near_order)
        return butterfly_sum(mine_sum, "narrow", nnarrow, narrow_order, BF)

    hdown = reduced(gdown, left_high, 4)
    hup = reduced(gup, left_high, 0)
    dx2, do, gwo, gg2 = run_resid(meta, x2, dn2, og, vec_all, mixed, own, first)
    hwo = reduced(gwo, left_low, 3)
    pq, pk, pv = run_attention_back(q, k, v, do, lse, cos, sin)
    gqkv = run_qkv_grad(n1, pq, pk, pv)
    hqkv = reduced(gqkv, left_low, 0)
    in_grad, ge, gg1 = run_input_grad(meta, tok, maskc, vec_all, dx2, pq, pk, pv, own, first)

    vec_grad = jnp.concatenate([ge, gg1, gg2, gbias[: FFB + 1]], axis=0)
    vec_grad = butterfly_sum(vec_grad, "narrow", nnarrow, narrow_order)
    vec_grad = butterfly_sum(vec_grad, "wide", nwide, wide_order)
    vec_owned = lax.dynamic_slice_in_dim(
        vec_grad.reshape(nnarrow, vectors.shape[0]), n, 1, axis=0
    )[0]

    turned = jnp.concatenate([hqkv, hwo, hup, hdown], axis=0)
    new_first, new_second, back = run_adam(own_blocks, turned, mom_first, mom_second, basis_right)
    backs = tree_gather(back, "wide", nwide, wide_order)
    new_weights = run_update(own_blocks, meta, weights, backs, left_low, left_high)

    vec_mean = BETA * vec_first + (1.0 - BETA) * vec_owned
    vec_square = BETA * vec_second + (1.0 - BETA) * vec_owned * vec_owned
    vec_new = vectors - RATE_VECTOR * vec_mean / (jnp.sqrt(vec_square) + EPS_ADAM)
    return (
        layer_out[None],
        in_grad[None],
        new_weights,
        new_first,
        new_second,
        vec_new,
        vec_mean,
        vec_square,
    )


def solution(mesh):
    return jax.shard_map(
        partial(on_device, mesh.shape["wide"], mesh.shape["narrow"]),
        mesh=mesh,
        in_specs=(
            P(("wide", "narrow"), None, None),
            P(("wide", "narrow"), None),
            P(("wide", "narrow"), None, None),
            P(),
            P("narrow", None, None),
            P("narrow"),
            P("narrow"),
            P("narrow"),
            P("narrow", "wide", None),
            P("narrow", "wide", None),
            P("narrow", None, "wide"),
            P("narrow", None, None),
        ),
        out_specs=(
            P(("wide", "narrow"), None, None),
            P(("wide", "narrow"), None, None),
            P("narrow", None, None),
            P("narrow", "wide", None),
            P("narrow", "wide", None),
            P("narrow"),
            P("narrow"),
            P("narrow"),
        ),
        check_vma=False,
    )
```

```python
from functools import partial
import math
from typing import NamedTuple

import jax
import jax.numpy as jnp
from jax import lax
from jax.experimental import pallas as pl
from jax.experimental.pallas import tpu as pltpu
from jax.sharding import PartitionSpec as P


D = 768
HEADS = 12
FF = 3072
BLK = 16
SEQ = 384
NBLK = 12
ROWS = 2 * SEQ
FFB = FF // D
PAIR = 128
NPAIR = D // PAIR
TILE = 128
CHUNK = 256

EPS_NORM = 1e-05
EPS_ADAM = 1e-08
RATE_MATRIX = 0.05
RATE_VECTOR = 0.3
BETA = 0.5
MASK_FILL = -1e30
GELU_A = math.sqrt(2.0 / math.pi)
GELU_B = 0.044715

BF = jnp.bfloat16
F32 = jnp.float32


NT = (((1,), (1,)), ((), ()))
TN = (((0,), (0,)), ((), ()))
NN = (((1,), (0,)), ((), ()))


def mm(a, b, dims=NN):
    return lax.dot_general(a, b, dims, preferred_element_type=F32)


def any_spec():
    return pl.BlockSpec(memory_space=pl.ANY)


class Group(NamedTuple):
    arrays: tuple
    where: tuple


def xor_permute(x, axis, size, mask):
    return lax.ppermute(x, axis, [(i, i ^ mask) for i in range(size)])


def far_bits(size):
    bits = []
    bit = size // 2
    while bit:
        bits.append(bit)
        bit //= 2
    return bits


def narrow_parts(x, size):
    have = {0: x}
    for bit in far_bits(size):
        fresh = {r | bit: xor_permute(have[r], "narrow", size, bit) for r in have}
        have.update(fresh)
    return [have[r] for r in range(size)]


def wide_group(x, size, order, merge):
    bufs = [(x[None], [0])]
    for i, bit in enumerate(order):
        fresh = [(xor_permute(a, "wide", size, bit), [r | bit for r in rels]) for a, rels in bufs]
        bufs = bufs + fresh
        if i < merge:
            bufs = [(jnp.concatenate([a for a, _ in bufs], axis=0), sum((r for _, r in bufs), []))]
    where = [None] * (2 ** len(order))
    for i, (_, rels) in enumerate(bufs):
        for j, r in enumerate(rels):
            where[r] = (i, j)
    return Group(tuple(a for a, _ in bufs), tuple(where))


def scatter_sum(keep, send, nwide, steps):
    parts = [keep, xor_permute(send, "wide", nwide, 1)]
    cur = keep.shape[0]
    for axis, size, bit in steps:
        half = cur // 2
        total = total_of([p[half:cur].astype(F32) for p in parts])
        got = xor_permute(total.astype(BF), axis, size, bit)
        parts = [p[:half] for p in parts] + [got]
        cur = half
    return total_of([p[0].astype(F32) for p in parts])


def butterfly_sum(x, axis, size, order, low=None):
    for bit in order:
        sent = x if low is None else x.astype(low)
        x = x + xor_permute(sent, axis, size, bit).astype(x.dtype)
    return x


def split_refs(groups, refs):
    out = []
    at = 0
    for arrays, where in groups:
        out.append((refs[at : at + arrays], where))
        at += arrays
    return out


def group_shapes(groups):
    return tuple((len(g.arrays), g.where) for g in groups)


def group_arrays(groups):
    return [a for g in groups for a in g.arrays]


def start_slices(group, index, dst, sem, me):
    refs, where = group
    count = len(where)
    rows = D // count
    base = me & (count - 1)
    for r, (i, j) in enumerate(where):
        at = pl.multiple_of((base ^ r) * rows, rows)
        pltpu.make_async_copy(refs[i].at[j, index], dst.at[pl.ds(at, rows)], sem).start()


def start_block(meta, block, own, groups, dst, sem):
    me = meta[0]
    source = meta[2 + block]
    index = meta[2 + NBLK + block]

    @pl.when(source == 0)
    def _():
        pltpu.make_async_copy(own.at[index], dst, sem).start()

    for k, group in enumerate(groups):

        @pl.when(source == k + 1)
        def _():
            start_slices(group, index, dst, sem, me)


def start_scatter(src, keep, send, item, steps, nwide, meta, sem):
    me = meta[0]
    rows = D // nwide
    side = (item & 1) ^ meta[1]
    for r in range(nwide):
        at = 0
        for axis, _, bit in steps:
            at = at * 2 + (side if axis == "narrow" else (1 if r & bit else 0))
        dst = send if r & 1 else keep
        row = pl.multiple_of((me ^ r) * rows, rows)
        pltpu.make_async_copy(src.at[pl.ds(row, rows)], dst.at[at, item // 2], sem).start()


def wait_block(dst, sem):
    pltpu.make_async_copy(dst, dst, sem).wait()


def norm_stats(z):
    mean = jnp.mean(z, axis=-1, keepdims=True)
    cen = z - mean
    var = jnp.mean(cen * cen, axis=-1, keepdims=True)
    return cen, lax.rsqrt(var + EPS_NORM)


def norm_back(zh, r, dz):
    return r * (
        dz
        - jnp.mean(dz, axis=-1, keepdims=True)
        - zh * jnp.mean(dz * zh, axis=-1, keepdims=True)
    )


def half_swap(z):
    lane = lax.broadcasted_iota(jnp.int32, z.shape, 1) % 64
    return jnp.where(lane < 32, pltpu.roll(z, PAIR - 32, 1), pltpu.roll(z, 32, 1))


def tile_masks():
    key = lax.broadcasted_iota(jnp.int32, (TILE, 2 * TILE), 0) // BLK
    qry = lax.broadcasted_iota(jnp.int32, (TILE, 2 * TILE), 1) % TILE // BLK
    return key == qry, key < qry, key <= qry


def head_split(x):
    lane = lax.broadcasted_iota(jnp.int32, x.shape, 1)
    zero = jnp.zeros_like(x)
    return jnp.concatenate([jnp.where(lane < 64, x, zero), jnp.where(lane < 64, zero, x)], axis=0)


def head_join(xt):
    row = lax.broadcasted_iota(jnp.int32, (PAIR, TILE), 0)
    return jnp.where(row < 64, xt[:, :TILE], xt[:, TILE:])


def key_parts(noised, t, masks):
    same, before, upto = masks
    parts = []
    if t > 0:
        parts.append((SEQ, TILE * t, None))
    parts.append((SEQ + TILE * t, TILE, before if noised else upto))
    if noised:
        parts.append((TILE * t, TILE, same))
    return parts


def masked_scores(k_ref, lanes, parts, qs):
    out = []
    for start, count, mask in parts:
        s = mm(k_ref[pl.ds(start, count), lanes], qs, NT)
        out.append(s if mask is None else jnp.where(mask, s, MASK_FILL))
    return out


def total_of(items):
    total = items[0]
    for x in items[1:]:
        total = total + x
    return total


def input_rows(tok_ref, mask_ref, vp_ref, half):
    tok = tok_ref[...].astype(F32)
    if half == 1:
        return tok
    return jnp.where(mask_ref[...] == 1, vp_ref[0:1, :], tok)


def forward_kernel(shapes, meta, tok, maskc, vp, cos, sin, own, *refs):
    nw = sum(n for n, _ in shapes)
    first = split_refs(shapes, refs)
    q_ref, k_ref, v_ref, n1_ref, o_ref, lse_ref, x2_ref, n2_ref = refs[nw : nw + 8]
    wbuf, sems = refs[nw + 8 :]
    for b in range(4):
        start_block(meta, b, own, first, wbuf.at[b], sems.at[b])
    for half in range(2):
        cen, r = norm_stats(input_rows(tok, maskc, vp, half))
        n1_ref[half * SEQ : (half + 1) * SEQ, :] = (cen * r * vp[1:2, :]).astype(BF)
    for b, out in enumerate((q_ref, k_ref, v_ref)):
        wait_block(wbuf.at[b], sems.at[b])
        for half in range(2):
            rows = slice(half * SEQ, (half + 1) * SEQ)
            for c in range(D // CHUNK):
                z = mm(n1_ref[rows, :], wbuf[b, :, c * CHUNK : (c + 1) * CHUNK])
                for s in range(CHUNK // PAIR):
                    piece = z[:, s * PAIR : (s + 1) * PAIR]
                    if b < 2:
                        piece = piece * cos[...] + half_swap(piece) * sin[...]
                    if b == 0:
                        piece = piece * 0.125
                    at = c * CHUNK + s * PAIR
                    out[rows, at : at + PAIR] = piece.astype(BF)

    masks = tile_masks()

    def one_pair(p, carry):
        lanes = pl.ds(pl.multiple_of(p * PAIR, PAIR), PAIR)
        for noised in (True, False):
            for t in range(SEQ // TILE):
                row = (0 if noised else SEQ) + TILE * t
                qs = head_split(q_ref[pl.ds(row, TILE), lanes])
                parts = key_parts(noised, t, masks)
                scores = masked_scores(k_ref, lanes, parts, qs)
                tops = [jnp.max(s, axis=0, keepdims=True) for s in scores]
                top = tops[0]
                for x in tops[1:]:
                    top = jnp.maximum(top, x)
                expo = [jnp.exp(s - top) for s in scores]
                total = total_of([jnp.sum(e, axis=0, keepdims=True) for e in expo])
                mixed = total_of(
                    [
                        mm(v_ref[pl.ds(start, count), lanes], e.astype(BF), TN)
                        for (start, count, _), e in zip(parts, expo)
                    ]
                )
                mixed = mixed * (1.0 / total)
                o_ref[pl.ds(row, TILE), lanes] = head_join(mixed).T.astype(BF)
                lse = top + jnp.log(total)
                lse_ref[p, 0:1, row : row + TILE] = lse[:, :TILE]
                lse_ref[p, 1:2, row : row + TILE] = lse[:, TILE:]
        return carry

    lax.fori_loop(0, NPAIR, one_pair, 0)
    wait_block(wbuf.at[3], sems.at[3])
    for half in range(2):
        rows = slice(half * SEQ, (half + 1) * SEQ)
        x2 = input_rows(tok, maskc, vp, half) + mm(o_ref[rows, :], wbuf[3])
        x2_ref[rows, :] = x2
        cen, r = norm_stats(x2)
        n2_ref[rows, :] = (cen * r * vp[2:3, :]).astype(BF)


def run_forward(meta, tok, maskc, vp, cos, sin, own, first):
    vm = pl.BlockSpec(memory_space=pltpu.VMEM)
    sq = jax.ShapeDtypeStruct((ROWS, D), BF)
    arrays = group_arrays(first)
    return pl.pallas_call(
        partial(forward_kernel, group_shapes(first)),
        name="forward_attention",
        out_shape=(
            sq,
            sq,
            sq,
            sq,
            sq,
            jax.ShapeDtypeStruct((NPAIR, 2, ROWS), F32),
            jax.ShapeDtypeStruct((ROWS, D), F32),
            sq,
        ),
        in_specs=[pl.BlockSpec(memory_space=pltpu.SMEM)] + [vm] * 5 + [any_spec()] * (1 + len(arrays)),
        out_specs=(vm,) * 8,
        scratch_shapes=[pltpu.VMEM((4, D, D), BF), pltpu.SemaphoreType.DMA((4,))],
    )(meta, tok, maskc, vp, cos, sin, own, *arrays)


def ffn_kernel(shapes, plans, nwide, meta, n2, og, x2, vp, own, *refs):
    nw = sum(n for n, _ in shapes)
    groups = split_refs(shapes, refs)
    layer_ref, up_keep, up_send, down_keep, down_send, dn2_ref, gbias_ref = refs[nw : nw + 7]
    wup, wdown, yacc, act, dhid, gup, gdown, sems, gsem = refs[nw + 7 :]
    f = pl.program_id(0)
    slot = f % 2

    @pl.when(f == 0)
    def _():
        for b in range(FFB):
            start_block(meta, 4 + b, own, groups, wup.at[b], sems.at[b])
            start_block(meta, 8 + b, own, groups, wdown.at[b], sems.at[4 + b])
        yacc[...] = jnp.zeros_like(yacc)
        dn2_ref[...] = jnp.zeros_like(dn2_ref)
        gbias_ref[FFB : FFB + 1, :] = jnp.sum(og[...].astype(F32), axis=0, keepdims=True)

    @pl.when(f > 1)
    def _():
        wait_block(gup.at[slot], gsem.at[slot])
        wait_block(gdown.at[slot], gsem.at[2 + slot])

    wait_block(wup.at[f], sems.at[f])
    wait_block(wdown.at[f], sems.at[4 + f])
    bias = vp[pl.ds(3 + f, 1), :]
    gb = jnp.zeros((1, D), F32)
    for c in range(ROWS // CHUNK):
        rows = slice(c * CHUNK, (c + 1) * CHUNK)
        h = mm(n2[rows, :], wup[f]) + bias
        hh = h * h
        th = jnp.tanh(h * (GELU_A + (GELU_A * GELU_B) * hh))
        lift = 0.5 + 0.5 * th
        slope = lift + (0.5 * h) * (1.0 - th * th) * (GELU_A + (3.0 * GELU_A * GELU_B) * hh)
        act[rows, :] = (h * lift).astype(BF)
        dh = mm(og[rows, :], wdown[f], NT) * slope
        gb = gb + jnp.sum(dh, axis=0, keepdims=True)
        dhid[rows, :] = dh.astype(BF)
        yacc[rows, :] += mm(act[rows, :], wdown[f])
        dn2_ref[rows, :] += mm(dhid[rows, :], wup[f], NT)
    gbias_ref[pl.ds(f, 1), :] = gb
    gdown[slot] = mm(og[...], act[...], TN).astype(BF)
    start_scatter(
        gdown.at[slot], down_keep, down_send, f, plans[1], nwide, meta, gsem.at[2 + slot]
    )
    gup[slot] = mm(dhid[...], n2[...], TN).astype(BF)
    start_scatter(gup.at[slot], up_keep, up_send, f, plans[0], nwide, meta, gsem.at[slot])

    @pl.when(f == FFB - 1)
    def _():
        layer_ref[...] = (x2[...] + yacc[...] + vp[7:8, :]).astype(BF)
        for k in range(2):
            wait_block(gup.at[k], gsem.at[k])
            wait_block(gdown.at[k], gsem.at[2 + k])


def scatter_shape(nwide, count):
    return jax.ShapeDtypeStruct((nwide, count // 2, D // nwide, D), BF)


def run_ffn(meta, n2, og, x2, vp, own, groups, plans, nwide):
    def whole(shape):
        return pl.BlockSpec(shape, lambda f: (0,) * len(shape))

    arrays = group_arrays(groups)
    part = scatter_shape(nwide, FFB)
    return pl.pallas_call(
        partial(ffn_kernel, group_shapes(groups), plans, nwide),
        name="feed_forward",
        grid=(FFB,),
        out_shape=(
            jax.ShapeDtypeStruct((ROWS, D), BF),
            part,
            part,
            part,
            part,
            jax.ShapeDtypeStruct((ROWS, D), F32),
            jax.ShapeDtypeStruct((8, D), F32),
        ),
        in_specs=[
            pl.BlockSpec(memory_space=pltpu.SMEM),
            whole((ROWS, D)),
            whole((ROWS, D)),
            whole((ROWS, D)),
            whole((8, D)),
        ]
        + [any_spec()] * (1 + len(arrays)),
        out_specs=(whole((ROWS, D)),) + (any_spec(),) * 4 + (whole((ROWS, D)), whole((8, D))),
        scratch_shapes=[
            pltpu.VMEM((FFB, D, D), BF),
            pltpu.VMEM((FFB, D, D), BF),
            pltpu.VMEM((ROWS, D), F32),
            pltpu.VMEM((ROWS, D), BF),
            pltpu.VMEM((ROWS, D), BF),
            pltpu.VMEM((2, D, D), BF),
            pltpu.VMEM((2, D, D), BF),
            pltpu.SemaphoreType.DMA((2 * FFB,)),
            pltpu.SemaphoreType.DMA((4,)),
        ],
    )(meta, n2, og, x2, vp, own, *arrays)


def resid_kernel(shapes, meta, x2, dn2, og, vp, o_ref, own, *refs):
    nw = sum(n for n, _ in shapes)
    first = split_refs(shapes, refs)
    dx2_ref, do_ref, gwo_ref, gg_ref = refs[nw : nw + 4]
    wbuf, dlow, sems = refs[nw + 4 :]
    start_block(meta, 3, own, first, wbuf, sems.at[0])
    gg = jnp.zeros((1, D), F32)
    for c in range(ROWS // CHUNK):
        rows = slice(c * CHUNK, (c + 1) * CHUNK)
        cen, r = norm_stats(x2[rows, :])
        zh = cen * r
        dn = dn2[rows, :]
        gg = gg + jnp.sum(dn * zh, axis=0, keepdims=True)
        dx = og[rows, :].astype(F32) + norm_back(zh, r, dn * vp[2:3, :])
        dx2_ref[rows, :] = dx
        dlow[rows, :] = dx.astype(BF)
    gg_ref[...] = gg
    gwo_ref[...] = mm(dlow[...], o_ref[...], TN).astype(BF)
    wait_block(wbuf, sems.at[0])
    do_ref[...] = mm(dlow[...], wbuf[...], NT).astype(BF)


def run_resid(meta, x2, dn2, og, vp, mixed, own, first):
    vm = pl.BlockSpec(memory_space=pltpu.VMEM)
    arrays = group_arrays(first)
    return pl.pallas_call(
        partial(resid_kernel, group_shapes(first)),
        name="residual_back",
        out_shape=(
            jax.ShapeDtypeStruct((ROWS, D), F32),
            jax.ShapeDtypeStruct((ROWS, D), BF),
            jax.ShapeDtypeStruct((D, D), BF),
            jax.ShapeDtypeStruct((1, D), F32),
        ),
        in_specs=[pl.BlockSpec(memory_space=pltpu.SMEM)] + [vm] * 5 + [any_spec()] * (1 + len(arrays)),
        out_specs=(vm,) * 4,
        scratch_shapes=[
            pltpu.VMEM((D, D), BF),
            pltpu.VMEM((ROWS, D), BF),
            pltpu.SemaphoreType.DMA((1,)),
        ],
    )(meta, x2, dn2, og, vp, mixed, own, *arrays)


def attention_back_kernel(q, k, v, do, lse_ref, cos, sin, pq, pk, pv, dk, dv):
    masks = tile_masks()

    def one_pair(p, carry):
        lanes = pl.ds(pl.multiple_of(p * PAIR, PAIR), PAIR)
        dk[...] = jnp.zeros_like(dk)
        dv[...] = jnp.zeros_like(dv)
        for noised in (True, False):
            for t in range(SEQ // TILE):
                row = (0 if noised else SEQ) + TILE * t
                qs = head_split(q[pl.ds(row, TILE), lanes])
                ds = head_split(do[pl.ds(row, TILE), lanes])
                lse = jnp.concatenate(
                    [lse_ref[p, 0:1, row : row + TILE], lse_ref[p, 1:2, row : row + TILE]], axis=1
                )
                parts = key_parts(noised, t, masks)
                probs = [jnp.exp(s - lse) for s in masked_scores(k, lanes, parts, qs)]
                prods = []
                for (start, count, _), e in zip(parts, probs):
                    prods.append(e * mm(v[pl.ds(start, count), lanes], ds, NT))
                    dv[start : start + count, :] += mm(e.astype(BF), ds)
                dot = total_of([jnp.sum(x, axis=0, keepdims=True) for x in prods])
                dq = None
                for (start, count, _), e, x in zip(parts, probs, prods):
                    g = (x - e * dot).astype(BF)
                    dk[start : start + count, :] += mm(g, qs)
                    one = mm(k[pl.ds(start, count), lanes], g, TN)
                    dq = one if dq is None else dq + one
                dq = head_join(dq).T * 0.125
                at = TILE * t
                turn = dq * cos[at : at + TILE, :] - half_swap(dq) * sin[at : at + TILE, :]
                pq[pl.ds(row, TILE), lanes] = turn.astype(BF)
        for half in range(2):
            rows = slice(half * SEQ, (half + 1) * SEQ)
            z = dk[rows, :]
            pk[rows, lanes] = (z * cos[...] - half_swap(z) * sin[...]).astype(BF)
            pv[rows, lanes] = dv[rows, :].astype(BF)
        return carry

    lax.fori_loop(0, NPAIR, one_pair, 0)


def run_attention_back(q, k, v, do, lse, cos, sin):
    vm = pl.BlockSpec(memory_space=pltpu.VMEM)
    sq = jax.ShapeDtypeStruct((ROWS, D), BF)
    return pl.pallas_call(
        attention_back_kernel,
        name="attention_back",
        out_shape=(sq, sq, sq),
        in_specs=[vm] * 7,
        out_specs=(vm,) * 3,
        scratch_shapes=[pltpu.VMEM((ROWS, PAIR), F32), pltpu.VMEM((ROWS, PAIR), F32)],
    )(q, k, v, do, lse, cos, sin)


def qkv_grad_kernel(plans, nwide, meta, n1, pq, pk, pv, gwo, *refs):
    outs = (refs[0:2], refs[2:4])
    res, sems = refs[4:]
    start_scatter(gwo, *outs[1], 1, plans[1], nwide, meta, sems.at[3])
    for i, x in enumerate((pq, pk, pv)):
        res[i] = mm(x[...], n1[...], TN).astype(BF)
        start_scatter(
            res.at[i], *outs[i // 2], i % 2, plans[i // 2], nwide, meta, sems.at[i]
        )
    for i in range(3):
        wait_block(res.at[i], sems.at[i])
    wait_block(gwo, sems.at[3])


def run_qkv_grad(meta, n1, pq, pk, pv, gwo, plans, nwide):
    vm = pl.BlockSpec(memory_space=pltpu.VMEM)
    return pl.pallas_call(
        partial(qkv_grad_kernel, plans, nwide),
        name="qkv_grad",
        out_shape=(scatter_shape(nwide, 2),) * 4,
        in_specs=[pl.BlockSpec(memory_space=pltpu.SMEM)] + [vm] * 5,
        out_specs=(any_spec(),) * 4,
        scratch_shapes=[pltpu.VMEM((3, D, D), BF), pltpu.SemaphoreType.DMA((4,))],
    )(meta, n1, pq, pk, pv, gwo)


def input_grad_kernel(shapes, meta, tok, maskc, vp, dx2, pq, pk, pv, own, *refs):
    nw = sum(n for n, _ in shapes)
    first = split_refs(shapes, refs)
    in_ref, ge_ref, gg_ref = refs[nw : nw + 3]
    wbuf, sems = refs[nw + 3 :]
    for b in range(3):
        start_block(meta, b, own, first, wbuf.at[b], sems.at[b])
    for b in range(3):
        wait_block(wbuf.at[b], sems.at[b])
    gg = jnp.zeros((1, D), F32)
    kept = None
    for half in range(2):
        rows = slice(half * SEQ, (half + 1) * SEQ)
        dn = total_of([mm(x[rows, :], wbuf[b], NT) for b, x in enumerate((pq, pk, pv))])
        cen, r = norm_stats(input_rows(tok, maskc, vp, half))
        zh = cen * r
        gg = gg + jnp.sum(dn * zh, axis=0, keepdims=True)
        dx = dx2[rows, :] + norm_back(zh, r, dn * vp[1:2, :])
        if half == 0:
            hit = maskc[...] == 1
            ge_ref[...] = jnp.sum(jnp.where(hit, dx, 0.0), axis=0, keepdims=True)
            kept = jnp.where(hit, 0.0, dx)
        else:
            in_ref[...] = (dx + kept).astype(BF)
    gg_ref[...] = gg


def run_input_grad(meta, tok, maskc, vp, dx2, pq, pk, pv, own, first):
    vm = pl.BlockSpec(memory_space=pltpu.VMEM)
    arrays = group_arrays(first)
    return pl.pallas_call(
        partial(input_grad_kernel, group_shapes(first)),
        name="input_grad",
        out_shape=(
            jax.ShapeDtypeStruct((SEQ, D), BF),
            jax.ShapeDtypeStruct((1, D), F32),
            jax.ShapeDtypeStruct((1, D), F32),
        ),
        in_specs=[pl.BlockSpec(memory_space=pltpu.SMEM)] + [vm] * 7 + [any_spec()] * (1 + len(arrays)),
        out_specs=(vm,) * 3,
        scratch_shapes=[pltpu.VMEM((3, D, D), BF), pltpu.SemaphoreType.DMA((3,))],
    )(meta, tok, maskc, vp, dx2, pq, pk, pv, own, *arrays)


def send_kernel(scalars, direct, tree, *outs):
    outs[0][...] = direct[...].astype(BF)
    if len(outs) > 1:
        outs[1][...] = tree[...].astype(BF)


def run_send(scalars, weights, nwide, at, count, tree_at, tree_count):
    rows = D // nwide
    outs = [jax.ShapeDtypeStruct((count, D // 2, D), BF)]
    specs = [pl.BlockSpec((1, D // 2, D), lambda s, sc: (s, 0, 0))]
    if tree_count:
        outs.append(jax.ShapeDtypeStruct((tree_count, rows, D), BF))
        specs.append(
            pl.BlockSpec((1, rows, D), lambda s, sc: (jnp.minimum(s, tree_count - 1), 0, 0))
        )
    return pl.pallas_call(
        send_kernel,
        name="send_weights",
        grid_spec=pltpu.PrefetchScalarGridSpec(
            num_scalar_prefetch=1,
            grid=(count,),
            in_specs=[
                pl.BlockSpec((1, D // 2, D), lambda s, sc: (sc[2 + at + s], sc[1], 0)),
                pl.BlockSpec(
                    (1, rows, D),
                    lambda s, sc: (sc[2 + tree_at + jnp.minimum(s, max(tree_count, 1) - 1)], sc[0], 0),
                ),
            ],
            out_specs=tuple(specs),
        ),
        out_shape=tuple(outs),
    )(scalars, weights, weights)


def turn_kernel(count, sizes, shapes, meta, items, slots, *refs):
    grads = refs[: len(sizes)]
    refs = refs[len(sizes) :]
    nw = sum(n for n, _ in shapes)
    (left,) = split_refs(shapes, refs)
    out = refs[nw]
    lbuf, gbuf, lsem, gsem = refs[nw + 1 :]
    for s in range(count):
        item = items[s]
        if len(grads) == 1:
            pltpu.make_async_copy(grads[0].at[item], gbuf.at[s], gsem.at[s]).start()
        else:

            @pl.when(item < sizes[0])
            def _():
                pltpu.make_async_copy(grads[0].at[item], gbuf.at[s], gsem.at[s]).start()

            @pl.when(item >= sizes[0])
            def _():
                pltpu.make_async_copy(
                    grads[1].at[item - sizes[0]], gbuf.at[s], gsem.at[s]
                ).start()

        start_slices(left, slots[s], lbuf.at[s], lsem.at[s], meta[0])
    parts = []
    for s in range(count):
        wait_block(gbuf.at[s], gsem.at[s])
        wait_block(lbuf.at[s], lsem.at[s])
        parts.append(mm(lbuf[s], gbuf[s], NT))
    out[...] = jnp.concatenate(parts, axis=1).astype(BF)


def run_turn(meta, items, slots, grads, left):
    count = items.shape[0]
    rows = grads[0].shape[1]
    sizes = tuple(g.shape[0] for g in grads)
    smem = pl.BlockSpec(memory_space=pltpu.SMEM)
    return pl.pallas_call(
        partial(turn_kernel, count, sizes, group_shapes([left])),
        name="gradient_turn",
        out_shape=jax.ShapeDtypeStruct((D, count * rows), BF),
        in_specs=[smem] * 3 + [any_spec()] * (len(grads) + len(left.arrays)),
        out_specs=pl.BlockSpec(memory_space=pltpu.VMEM),
        scratch_shapes=[
            pltpu.VMEM((count, D, D), BF),
            pltpu.VMEM((count, rows, D), BF),
            pltpu.SemaphoreType.DMA((count,)),
            pltpu.SemaphoreType.DMA((count,)),
        ],
    )(meta, items, slots, *grads, *left.arrays)


def adam_kernel(count, chained, slots, live, grads, first, second, right, *refs):
    nf, ns, back, full = refs[2 if chained else 0 :]
    s = pl.program_id(0)
    rows = first.shape[1]

    @pl.when(s == 0)
    def _():
        for k in range(count):
            for src in range(D // rows):
                at = slice(src * rows, (src + 1) * rows)
                full[k, :, at] = grads[at, k * rows : (k + 1) * rows].astype(F32)

    @pl.when(live[s] == 1)
    def _():
        basis = right[0].astype(BF)
        turned = mm(full[s].astype(BF), basis)
        one = BETA * first[0] + (1.0 - BETA) * turned
        two = BETA * second[0] + (1.0 - BETA) * turned * turned
        nf[0] = one
        ns[0] = two
        step = one / (jnp.sqrt(two) + EPS_ADAM)
        back[0] = mm(step.astype(BF), basis, NT).astype(BF)

    @pl.when(live[s] == 0)
    def _():
        nf[...] = jnp.zeros_like(nf)
        ns[...] = jnp.zeros_like(ns)
        back[...] = jnp.zeros_like(back)


def run_adam(slots, live, grads, first, second, right, earlier):
    count = slots.shape[0]
    rows = first.shape[1]
    state = pl.BlockSpec((1, rows, D), lambda s, slots, live: (slots[s], 0, 0))
    return pl.pallas_call(
        partial(adam_kernel, count, bool(earlier)),
        name="adam_step",
        grid_spec=pltpu.PrefetchScalarGridSpec(
            num_scalar_prefetch=2,
            grid=(count,),
            in_specs=[
                pl.BlockSpec(grads.shape, lambda s, *_: (0, 0)),
                state,
                state,
                pl.BlockSpec((1, D, D), lambda s, slots, live: (slots[s], 0, 0)),
            ]
            + [any_spec()] * len(earlier),
            out_specs=(state, state, pl.BlockSpec((1, rows, D), lambda s, *_: (s, 0, 0))),
            scratch_shapes=[pltpu.VMEM((count, rows, D), F32)],
        ),
        out_shape=(
            jax.ShapeDtypeStruct(first.shape, F32),
            jax.ShapeDtypeStruct(first.shape, F32),
            jax.ShapeDtypeStruct((count, rows, D), BF),
        ),
        input_output_aliases={6: 0, 7: 1} if earlier else {},
    )(slots, live, grads, first, second, right, *earlier)


def update_kernel(shapes, half, chained, slots, live, meta, weights, *refs):
    nw = sum(n for n, _ in shapes)
    back_a, back_b, left = split_refs(shapes, refs)
    out, lbuf, bbuf, lsem, bsem = refs[nw + (1 if chained else 0) :]
    s = pl.program_id(0)
    count = pl.num_programs(0)
    me = meta[0]
    slot = s % 2

    def begin(item, where):
        @pl.when(live[item] == 1)
        def _():
            @pl.when(item < half)
            def _():
                start_slices(back_a, item, bbuf.at[where], bsem.at[where], me)

            @pl.when(item >= half)
            def _():
                start_slices(back_b, item - half, bbuf.at[where], bsem.at[where], me)

            start_slices(left, slots[item], lbuf.at[where], lsem.at[where], me)

    @pl.when(s == 0)
    def _():
        begin(0, 0)

    @pl.when(s + 1 < count)
    def _():
        begin(s + 1, 1 - slot)

    @pl.when(live[s] == 1)
    def _():
        wait_block(lbuf.at[slot], lsem.at[slot])
        wait_block(bbuf.at[slot], bsem.at[slot])
        out[0] = weights[0] - RATE_MATRIX * mm(lbuf[slot], bbuf[slot], TN)

    @pl.when(live[s] == 0)
    def _():
        out[...] = jnp.zeros_like(out)


def run_update(slots, live, meta, weights, backs, half, left, earlier):
    groups = backs + [left]
    arrays = group_arrays(groups)
    whole = pl.BlockSpec((1, D, D), lambda s, slots, *_: (slots[s], 0, 0))
    return pl.pallas_call(
        partial(update_kernel, group_shapes(groups), half, bool(earlier)),
        name="weight_update",
        grid_spec=pltpu.PrefetchScalarGridSpec(
            num_scalar_prefetch=3,
            grid=(slots.shape[0],),
            in_specs=[whole] + [any_spec()] * (len(arrays) + len(earlier)),
            out_specs=whole,
            scratch_shapes=[
                pltpu.VMEM((2, D, D), BF),
                pltpu.VMEM((2, D, D), BF),
                pltpu.SemaphoreType.DMA((2,)),
                pltpu.SemaphoreType.DMA((2,)),
            ],
        ),
        out_shape=jax.ShapeDtypeStruct(weights.shape, F32),
        input_output_aliases={4 + len(arrays): 0} if earlier else {},
    )(slots, live, meta, weights, *arrays, *earlier)


def rotary_tables():
    half_size = D // HEADS // 2
    position_col = jnp.arange(SEQ, dtype=jnp.int32).astype(F32)
    frequency = jnp.exp(
        jnp.arange(half_size, dtype=F32) * (-2.0 * math.log(10000.0) / (2 * half_size))
    )
    angles = position_col[:, None] * frequency[None, :]
    cosine = jnp.cos(angles)
    sine = jnp.sin(angles)
    return (
        jnp.concatenate([cosine, cosine, cosine, cosine], axis=1),
        jnp.concatenate([-sine, sine, -sine, sine], axis=1),
    )


def on_device(nwide, nnarrow, *args):
    return whole_step(nwide, nnarrow, *args)


def whole_step(
    nwide,
    nnarrow,
    tokens,
    masked,
    out_grad,
    slot_block,
    weights,
    vectors,
    vec_first,
    vec_second,
    mom_first,
    mom_second,
    basis_left,
    basis_right,
):
    sd = weights.shape[0]
    slots = sd * nnarrow
    w = lax.axis_index("wide").astype(jnp.int32)
    n = lax.axis_index("narrow").astype(jnp.int32)
    top = nnarrow // 2
    nbit = n // top
    far_order = far_bits(nwide)
    left_order = far_order[:1] + far_order[-2:-1] + far_order[1:-2] + far_order[-1:]
    inner = [("wide", nwide, bit) for bit in far_order[-2::-1]]
    split = [("narrow", nnarrow, top)]
    near_x = tuple(split + inner)
    near_y = tuple(inner[:1] + split + inner[1:])

    ids = jnp.arange(slots, dtype=jnp.int32)
    hits = slot_block[None, :] == jnp.arange(NBLK, dtype=jnp.int32)[:, None]
    block_slot = jnp.sum(jnp.where(hits, ids[None, :], 0), axis=1)
    earlier = (
        (slot_block[None, :] < slot_block[:, None])
        | ((slot_block[None, :] == slot_block[:, None]) & (ids[None, :] < ids[:, None]))
    ) & (ids[None, :] // sd == ids[:, None] // sd)
    slot_rank = jnp.sum(earlier.astype(jnp.int32), axis=1)
    block_rank = jnp.sum(jnp.where(hits, slot_rank[None, :], 0), axis=1)
    own_blocks = lax.dynamic_slice_in_dim(slot_block, n * sd, sd)
    own_rank = lax.dynamic_slice_in_dim(slot_rank, n * sd, sd)
    at_rank = own_rank[None, :] == jnp.arange(sd, dtype=jnp.int32)[:, None]
    sorted_slots = jnp.sum(
        jnp.where(at_rank, jnp.arange(sd, dtype=jnp.int32)[None, :], 0), axis=1
    )
    sorted_blocks = jnp.sum(jnp.where(at_rank, own_blocks[None, :], 0), axis=1)
    sorted_live = (sorted_blocks < NBLK).astype(jnp.int32)

    scalars = jnp.concatenate([w[None], (w & 1)[None], sorted_slots]).astype(jnp.int32)
    c1 = min(4, sd)
    d1 = c1 // 2
    pieces = [("d1", 0, d1, True), ("t1", d1, c1 - d1, False)]
    if sd > c1:
        mid = (sd - c1) // 2
        pieces += [("d2", c1, mid, True), ("t2", c1 + mid, sd - c1 - mid, False)]

    def spread(x, direct):
        got = narrow_parts(x, nnarrow)[1:]
        got = got[0] if len(got) == 1 else jnp.concatenate(got, axis=0)
        if direct:
            return wide_group(got, nwide, [1], 0)
        return wide_group(got, nwide, far_order, len(far_order) - 2)

    direct, tree = run_send(scalars, weights, nwide, 0, d1, d1, c1 - d1)
    early_tree = spread(tree, False)
    early_direct = spread(direct, True)
    first = [early_direct, early_tree]
    groups = list(first)
    if sd > c1:
        direct, tree = run_send(scalars, weights, nwide, c1, mid, c1 + mid, sd - c1 - mid)
        groups += [spread(direct, True), spread(tree, False)]
    own = weights.astype(BF)

    far = n ^ (block_slot // sd)
    source = jnp.zeros((NBLK,), jnp.int32)
    index = block_slot % sd
    for k, (_, at, count, _) in enumerate(pieces):
        here = (far > 0) & (block_rank >= at) & (block_rank < at + count)
        source = jnp.where(here, k + 1, source)
        index = jnp.where(here, (far - 1) * count + block_rank - at, index)
    meta = jnp.concatenate([w[None], nbit[None], source, index]).astype(jnp.int32)

    vec_rel = jnp.stack(narrow_parts(vectors.astype(BF), nnarrow))
    vec_all = vec_rel[n ^ jnp.arange(nnarrow, dtype=jnp.int32)].reshape(8, D).astype(F32)

    left = wide_group(
        basis_left.transpose(0, 2, 1).astype(BF), nwide, left_order, len(left_order) - 2
    )

    cos, sin = rotary_tables()
    tok = tokens[0]
    maskc = masked[0][:, None]
    og = out_grad[0]

    q, k, v, n1, mixed, lse, x2, n2 = run_forward(meta, tok, maskc, vec_all, cos, sin, own, first)
    layer_out, up_keep, up_send, down_keep, down_send, dn2, gbias = run_ffn(
        meta, n2, og, x2, vec_all, own, groups, (near_y, near_x), nwide
    )

    def reduced(keep, send, steps):
        total = scatter_sum(keep, send, nwide, steps)
        rest = far_bits(nnarrow)[1:]
        total = butterfly_sum(total, "narrow", nnarrow, rest, BF).astype(BF)
        return [total, xor_permute(total, "narrow", nnarrow, top)]

    gdown = reduced(down_keep, down_send, near_x)
    gup = reduced(up_keep, up_send, near_y)
    dx2, do, gwo, gg2 = run_resid(meta, x2, dn2, og, vec_all, mixed, own, first)
    pq, pk, pv = run_attention_back(q, k, v, do, lse, cos, sin)
    qk_keep, qk_send, vo_keep, vo_send = run_qkv_grad(
        meta, n1, pq, pk, pv, gwo, (near_x, near_y), nwide
    )
    gqk = reduced(qk_keep, qk_send, near_x)
    gvo = reduced(vo_keep, vo_send, near_y)
    in_grad, ge, gg1 = run_input_grad(
        meta, tok, maskc, vec_all, dx2, pq, pk, pv, own, first
    )

    chunks = [(0, c1, 0)]
    if sd > c1:
        chunks = [(c1, sd, 4)] + chunks
    state = ()
    fresh = ()
    ffn_grads = jnp.concatenate(gup + gdown, axis=0)
    att_grads = jnp.concatenate(gqk + gvo, axis=0)
    for lo, hi, base in chunks:
        grads = [ffn_grads] if base else [att_grads, ffn_grads]
        block = jnp.clip(sorted_blocks[lo:hi], base, NBLK - 1)
        width = jnp.where(block < 4, 1, 2)
        start = jnp.where(block < 4, block // 2 * 2, block // 4 * 4)
        items = start - base + ((block & 1) ^ nbit) * width + (block - start) // 2
        held = sorted_slots[lo:hi]
        live = sorted_live[lo:hi]
        turned = run_turn(meta, items, held, grads, left)
        turned = lax.all_to_all(turned, "wide", 0, 0, tiled=True)
        *state, back = run_adam(
            held, live, turned, mom_first, mom_second, basis_right, state
        )
        half = (hi - lo + 1) // 2
        merge = len(far_order) - 2
        backs = [
            wide_group(back[:half], nwide, far_order, merge),
            wide_group(back[half:], nwide, left_order, merge),
        ]
        fresh = (run_update(held, live, meta, weights, backs, half, left, fresh),)
    new_first, new_second = state
    new_weights = fresh[0]

    vec_grad = jnp.concatenate([ge, gg1, gg2, gbias[: FFB + 1]], axis=0)
    vec_grad = butterfly_sum(vec_grad, "narrow", nnarrow, far_bits(nnarrow))
    vec_grad = butterfly_sum(vec_grad, "wide", nwide, far_order[:-1])
    vec_grad = butterfly_sum(vec_grad, "wide", nwide, far_order[-1:])
    vec_owned = lax.dynamic_slice_in_dim(
        vec_grad.reshape(nnarrow, vectors.shape[0]), n, 1, axis=0
    )[0]
    vec_mean = BETA * vec_first + (1.0 - BETA) * vec_owned
    vec_square = BETA * vec_second + (1.0 - BETA) * vec_owned * vec_owned
    vec_new = vectors - RATE_VECTOR * vec_mean / (jnp.sqrt(vec_square) + EPS_ADAM)
    return (
        layer_out[None],
        in_grad[None],
        new_weights,
        new_first,
        new_second,
        vec_new,
        vec_mean,
        vec_square,
    )


def solution(mesh):
    return jax.shard_map(
        partial(on_device, mesh.shape["wide"], mesh.shape["narrow"]),
        mesh=mesh,
        in_specs=(
            P(("wide", "narrow"), None, None),
            P(("wide", "narrow"), None),
            P(("wide", "narrow"), None, None),
            P(),
            P("narrow", None, None),
            P("narrow"),
            P("narrow"),
            P("narrow"),
            P("narrow", "wide", None),
            P("narrow", "wide", None),
            P("narrow", None, "wide"),
            P("narrow", None, None),
        ),
        out_specs=(
            P(("wide", "narrow"), None, None),
            P(("wide", "narrow"), None, None),
            P("narrow", None, None),
            P("narrow", "wide", None),
            P("narrow", "wide", None),
            P("narrow"),
            P("narrow"),
            P("narrow"),
        ),
        check_vma=False,
    )
```

```python
from functools import partial
import math
from typing import NamedTuple

import jax
import jax.numpy as jnp
from jax import lax
from jax.experimental import pallas as pl
from jax.experimental.pallas import tpu as pltpu
from jax.sharding import PartitionSpec as P


D = 768
HEADS = 12
FF = 3072
BLK = 16
SEQ = 384
NBLK = 12
ROWS = 2 * SEQ
FFB = FF // D
PAIR = 128
NPAIR = D // PAIR
TILE = 128
CHUNK = 256

EPS_NORM = 1e-05
EPS_ADAM = 1e-08
RATE_MATRIX = 0.05
RATE_VECTOR = 0.3
BETA = 0.5
MASK_FILL = -1e30
GELU_A = math.sqrt(2.0 / math.pi)
GELU_B = 0.044715

BF = jnp.bfloat16
F32 = jnp.float32


NT = (((1,), (1,)), ((), ()))
TN = (((0,), (0,)), ((), ()))
NN = (((1,), (0,)), ((), ()))


def mm(a, b, dims=NN):
    return lax.dot_general(a, b, dims, preferred_element_type=F32)


def any_spec():
    return pl.BlockSpec(memory_space=pl.ANY)


class Group(NamedTuple):
    arrays: tuple
    where: tuple


def xor_permute(x, axis, size, mask):
    return lax.ppermute(x, axis, [(i, i ^ mask) for i in range(size)])


def far_bits(size):
    bits = []
    bit = size // 2
    while bit:
        bits.append(bit)
        bit //= 2
    return bits


def narrow_parts(x, size):
    have = {0: x}
    for bit in far_bits(size):
        fresh = {r | bit: xor_permute(have[r], "narrow", size, bit) for r in have}
        have.update(fresh)
    return [have[r] for r in range(size)]


def wide_group(x, size, order, merge):
    bufs = [(x[None], [0])]
    for i, bit in enumerate(order):
        fresh = [(xor_permute(a, "wide", size, bit), [r | bit for r in rels]) for a, rels in bufs]
        bufs = bufs + fresh
        if i < merge:
            bufs = [(jnp.concatenate([a for a, _ in bufs], axis=0), sum((r for _, r in bufs), []))]
    where = [None] * (2 ** len(order))
    for i, (_, rels) in enumerate(bufs):
        for j, r in enumerate(rels):
            where[r] = (i, j)
    return Group(tuple(a for a, _ in bufs), tuple(where))


def scatter_sum(keep, send, nwide, steps):
    parts = [keep, xor_permute(send, "wide", nwide, 1)]
    cur = keep.shape[0]
    for axis, size, bit in steps:
        half = cur // 2
        total = total_of([p[half:cur].astype(F32) for p in parts])
        got = xor_permute(total.astype(BF), axis, size, bit)
        parts = [p[:half] for p in parts] + [got]
        cur = half
    return total_of([p[0].astype(F32) for p in parts])


def butterfly_sum(x, axis, size, order, low=None):
    for bit in order:
        sent = x if low is None else x.astype(low)
        x = x + xor_permute(sent, axis, size, bit).astype(x.dtype)
    return x


def split_refs(groups, refs):
    out = []
    at = 0
    for arrays, where in groups:
        out.append((refs[at : at + arrays], where))
        at += arrays
    return out


def group_shapes(groups):
    return tuple((len(g.arrays), g.where) for g in groups)


def group_arrays(groups):
    return [a for g in groups for a in g.arrays]


def start_slices(group, index, dst, sem, me):
    refs, where = group
    count = len(where)
    rows = D // count
    base = me & (count - 1)
    for r, (i, j) in enumerate(where):
        at = pl.multiple_of((base ^ r) * rows, rows)
        pltpu.make_async_copy(refs[i].at[j, index], dst.at[pl.ds(at, rows)], sem).start()


def start_block(meta, block, own, groups, dst, sem):
    me = meta[0]
    source = meta[2 + block]
    index = meta[2 + NBLK + block]

    @pl.when(source == 0)
    def _():
        pltpu.make_async_copy(own.at[index], dst, sem).start()

    for k, group in enumerate(groups):

        @pl.when(source == k + 1)
        def _():
            start_slices(group, index, dst, sem, me)


def start_scatter(src, keep, send, item, steps, nwide, meta, sem):
    me = meta[0]
    rows = D // nwide
    side = (item & 1) ^ meta[1]
    for r in range(nwide):
        at = 0
        for axis, _, bit in steps:
            at = at * 2 + (side if axis == "narrow" else (1 if r & bit else 0))
        dst = send if r & 1 else keep
        row = pl.multiple_of((me ^ r) * rows, rows)
        pltpu.make_async_copy(src.at[pl.ds(row, rows)], dst.at[at, item // 2], sem).start()


def wait_block(dst, sem):
    pltpu.make_async_copy(dst, dst, sem).wait()


def norm_stats(z):
    mean = jnp.mean(z, axis=-1, keepdims=True)
    cen = z - mean
    var = jnp.mean(cen * cen, axis=-1, keepdims=True)
    return cen, lax.rsqrt(var + EPS_NORM)


def norm_back(zh, r, dz):
    return r * (
        dz
        - jnp.mean(dz, axis=-1, keepdims=True)
        - zh * jnp.mean(dz * zh, axis=-1, keepdims=True)
    )


def half_swap(z):
    lane = lax.broadcasted_iota(jnp.int32, z.shape, 1) % 64
    return jnp.where(lane < 32, pltpu.roll(z, PAIR - 32, 1), pltpu.roll(z, 32, 1))


def tile_masks():
    key = lax.broadcasted_iota(jnp.int32, (TILE, 2 * TILE), 0) // BLK
    qry = lax.broadcasted_iota(jnp.int32, (TILE, 2 * TILE), 1) % TILE // BLK
    return key == qry, key < qry, key <= qry


def head_split(x):
    lane = lax.broadcasted_iota(jnp.int32, x.shape, 1)
    zero = jnp.zeros_like(x)
    return jnp.concatenate([jnp.where(lane < 64, x, zero), jnp.where(lane < 64, zero, x)], axis=0)


def head_join(xt):
    row = lax.broadcasted_iota(jnp.int32, (PAIR, TILE), 0)
    return jnp.where(row < 64, xt[:, :TILE], xt[:, TILE:])


def key_parts(noised, t, masks):
    same, before, upto = masks
    parts = []
    if t > 0:
        parts.append((SEQ, TILE * t, None))
    parts.append((SEQ + TILE * t, TILE, before if noised else upto))
    if noised:
        parts.append((TILE * t, TILE, same))
    return parts


def masked_scores(k_ref, lanes, parts, qs):
    out = []
    for start, count, mask in parts:
        s = mm(k_ref[pl.ds(start, count), lanes], qs, NT)
        out.append(s if mask is None else jnp.where(mask, s, MASK_FILL))
    return out


def total_of(items):
    total = items[0]
    for x in items[1:]:
        total = total + x
    return total


def input_rows(tok_ref, mask_ref, vp_ref, half):
    tok = tok_ref[...].astype(F32)
    if half == 1:
        return tok
    return jnp.where(mask_ref[...] == 1, vp_ref[0:1, :], tok)


def forward_kernel(shapes, meta, tok, maskc, vp, cos, sin, own, *refs):
    nw = sum(n for n, _ in shapes)
    first = split_refs(shapes, refs)
    q_ref, k_ref, v_ref, n1_ref, o_ref, lse_ref, x2_ref, n2_ref = refs[nw : nw + 8]
    wbuf, sems = refs[nw + 8 :]
    for b in range(4):
        start_block(meta, b, own, first, wbuf.at[b], sems.at[b])
    for half in range(2):
        cen, r = norm_stats(input_rows(tok, maskc, vp, half))
        n1_ref[half * SEQ : (half + 1) * SEQ, :] = (cen * r * vp[1:2, :]).astype(BF)
    for b, out in enumerate((q_ref, k_ref, v_ref)):
        wait_block(wbuf.at[b], sems.at[b])
        for half in range(2):
            rows = slice(half * SEQ, (half + 1) * SEQ)
            for c in range(D // CHUNK):
                z = mm(n1_ref[rows, :], wbuf[b, :, c * CHUNK : (c + 1) * CHUNK])
                for s in range(CHUNK // PAIR):
                    piece = z[:, s * PAIR : (s + 1) * PAIR]
                    if b < 2:
                        piece = piece * cos[...] + half_swap(piece) * sin[...]
                    if b == 0:
                        piece = piece * 0.125
                    at = c * CHUNK + s * PAIR
                    out[rows, at : at + PAIR] = piece.astype(BF)

    masks = tile_masks()

    def one_pair(p, carry):
        lanes = pl.ds(pl.multiple_of(p * PAIR, PAIR), PAIR)
        for noised in (True, False):
            for t in range(SEQ // TILE):
                row = (0 if noised else SEQ) + TILE * t
                qs = head_split(q_ref[pl.ds(row, TILE), lanes])
                parts = key_parts(noised, t, masks)
                scores = masked_scores(k_ref, lanes, parts, qs)
                tops = [jnp.max(s, axis=0, keepdims=True) for s in scores]
                top = tops[0]
                for x in tops[1:]:
                    top = jnp.maximum(top, x)
                expo = [jnp.exp(s - top) for s in scores]
                total = total_of([jnp.sum(e, axis=0, keepdims=True) for e in expo])
                mixed = total_of(
                    [
                        mm(v_ref[pl.ds(start, count), lanes], e.astype(BF), TN)
                        for (start, count, _), e in zip(parts, expo)
                    ]
                )
                mixed = mixed * (1.0 / total)
                o_ref[pl.ds(row, TILE), lanes] = head_join(mixed).T.astype(BF)
                lse = top + jnp.log(total)
                lse_ref[p, 0:1, row : row + TILE] = lse[:, :TILE]
                lse_ref[p, 1:2, row : row + TILE] = lse[:, TILE:]
        return carry

    lax.fori_loop(0, NPAIR, one_pair, 0)
    wait_block(wbuf.at[3], sems.at[3])
    for half in range(2):
        rows = slice(half * SEQ, (half + 1) * SEQ)
        x2 = input_rows(tok, maskc, vp, half) + mm(o_ref[rows, :], wbuf[3])
        x2_ref[rows, :] = x2
        cen, r = norm_stats(x2)
        n2_ref[rows, :] = (cen * r * vp[2:3, :]).astype(BF)


def run_forward(meta, tok, maskc, vp, cos, sin, own, first):
    vm = pl.BlockSpec(memory_space=pltpu.VMEM)
    sq = jax.ShapeDtypeStruct((ROWS, D), BF)
    arrays = group_arrays(first)
    return pl.pallas_call(
        partial(forward_kernel, group_shapes(first)),
        name="forward_attention",
        out_shape=(
            sq,
            sq,
            sq,
            sq,
            sq,
            jax.ShapeDtypeStruct((NPAIR, 2, ROWS), F32),
            jax.ShapeDtypeStruct((ROWS, D), F32),
            sq,
        ),
        in_specs=[pl.BlockSpec(memory_space=pltpu.SMEM)] + [vm] * 5 + [any_spec()] * (1 + len(arrays)),
        out_specs=(vm,) * 8,
        scratch_shapes=[pltpu.VMEM((4, D, D), BF), pltpu.SemaphoreType.DMA((4,))],
    )(meta, tok, maskc, vp, cos, sin, own, *arrays)


def ffn_kernel(shapes, plans, nwide, meta, n2, og, x2, vp, own, *refs):
    nw = sum(n for n, _ in shapes)
    groups = split_refs(shapes, refs)
    layer_ref, up_keep, up_send, down_keep, down_send, dn2_ref, gbias_ref = refs[nw : nw + 7]
    wup, wdown, yacc, act, dhid, gup, gdown, sems, gsem = refs[nw + 7 :]
    f = pl.program_id(0)
    slot = f % 2

    @pl.when(f == 0)
    def _():
        for b in range(FFB):
            start_block(meta, 4 + b, own, groups, wup.at[b], sems.at[b])
            start_block(meta, 8 + b, own, groups, wdown.at[b], sems.at[4 + b])
        yacc[...] = jnp.zeros_like(yacc)
        dn2_ref[...] = jnp.zeros_like(dn2_ref)
        gbias_ref[FFB : FFB + 1, :] = jnp.sum(og[...].astype(F32), axis=0, keepdims=True)

    @pl.when(f > 1)
    def _():
        wait_block(gup.at[slot], gsem.at[slot])
        wait_block(gdown.at[slot], gsem.at[2 + slot])

    wait_block(wup.at[f], sems.at[f])
    wait_block(wdown.at[f], sems.at[4 + f])
    bias = vp[pl.ds(3 + f, 1), :]
    gb = jnp.zeros((1, D), F32)
    for c in range(ROWS // CHUNK):
        rows = slice(c * CHUNK, (c + 1) * CHUNK)
        h = mm(n2[rows, :], wup[f]) + bias
        hh = h * h
        th = jnp.tanh(h * (GELU_A + (GELU_A * GELU_B) * hh))
        lift = 0.5 + 0.5 * th
        slope = lift + (0.5 * h) * (1.0 - th * th) * (GELU_A + (3.0 * GELU_A * GELU_B) * hh)
        act[rows, :] = (h * lift).astype(BF)
        dh = mm(og[rows, :], wdown[f], NT) * slope
        gb = gb + jnp.sum(dh, axis=0, keepdims=True)
        dhid[rows, :] = dh.astype(BF)
        yacc[rows, :] += mm(act[rows, :], wdown[f])
        dn2_ref[rows, :] += mm(dhid[rows, :], wup[f], NT)
    gbias_ref[pl.ds(f, 1), :] = gb
    gdown[slot] = mm(og[...], act[...], TN).astype(BF)
    start_scatter(
        gdown.at[slot], down_keep, down_send, f, plans[1], nwide, meta, gsem.at[2 + slot]
    )
    gup[slot] = mm(dhid[...], n2[...], TN).astype(BF)
    start_scatter(gup.at[slot], up_keep, up_send, f, plans[0], nwide, meta, gsem.at[slot])

    @pl.when(f == FFB - 1)
    def _():
        layer_ref[...] = (x2[...] + yacc[...] + vp[7:8, :]).astype(BF)
        for k in range(2):
            wait_block(gup.at[k], gsem.at[k])
            wait_block(gdown.at[k], gsem.at[2 + k])


def scatter_shape(nwide, count):
    return jax.ShapeDtypeStruct((nwide, count // 2, D // nwide, D), BF)


def run_ffn(meta, n2, og, x2, vp, own, groups, plans, nwide):
    def whole(shape):
        return pl.BlockSpec(shape, lambda f: (0,) * len(shape))

    arrays = group_arrays(groups)
    part = scatter_shape(nwide, FFB)
    return pl.pallas_call(
        partial(ffn_kernel, group_shapes(groups), plans, nwide),
        name="feed_forward",
        grid=(FFB,),
        out_shape=(
            jax.ShapeDtypeStruct((ROWS, D), BF),
            part,
            part,
            part,
            part,
            jax.ShapeDtypeStruct((ROWS, D), F32),
            jax.ShapeDtypeStruct((8, D), F32),
        ),
        in_specs=[
            pl.BlockSpec(memory_space=pltpu.SMEM),
            whole((ROWS, D)),
            whole((ROWS, D)),
            whole((ROWS, D)),
            whole((8, D)),
        ]
        + [any_spec()] * (1 + len(arrays)),
        out_specs=(whole((ROWS, D)),) + (any_spec(),) * 4 + (whole((ROWS, D)), whole((8, D))),
        scratch_shapes=[
            pltpu.VMEM((FFB, D, D), BF),
            pltpu.VMEM((FFB, D, D), BF),
            pltpu.VMEM((ROWS, D), F32),
            pltpu.VMEM((ROWS, D), BF),
            pltpu.VMEM((ROWS, D), BF),
            pltpu.VMEM((2, D, D), BF),
            pltpu.VMEM((2, D, D), BF),
            pltpu.SemaphoreType.DMA((2 * FFB,)),
            pltpu.SemaphoreType.DMA((4,)),
        ],
    )(meta, n2, og, x2, vp, own, *arrays)


def resid_kernel(shapes, meta, x2, dn2, og, vp, o_ref, own, *refs):
    nw = sum(n for n, _ in shapes)
    first = split_refs(shapes, refs)
    dx2_ref, do_ref, gwo_ref, gg_ref = refs[nw : nw + 4]
    wbuf, dlow, sems = refs[nw + 4 :]
    start_block(meta, 3, own, first, wbuf, sems.at[0])
    gg = jnp.zeros((1, D), F32)
    for c in range(ROWS // CHUNK):
        rows = slice(c * CHUNK, (c + 1) * CHUNK)
        cen, r = norm_stats(x2[rows, :])
        zh = cen * r
        dn = dn2[rows, :]
        gg = gg + jnp.sum(dn * zh, axis=0, keepdims=True)
        dx = og[rows, :].astype(F32) + norm_back(zh, r, dn * vp[2:3, :])
        dx2_ref[rows, :] = dx
        dlow[rows, :] = dx.astype(BF)
    gg_ref[...] = gg
    gwo_ref[...] = mm(dlow[...], o_ref[...], TN).astype(BF)
    wait_block(wbuf, sems.at[0])
    do_ref[...] = mm(dlow[...], wbuf[...], NT).astype(BF)


def run_resid(meta, x2, dn2, og, vp, mixed, own, first):
    vm = pl.BlockSpec(memory_space=pltpu.VMEM)
    arrays = group_arrays(first)
    return pl.pallas_call(
        partial(resid_kernel, group_shapes(first)),
        name="residual_back",
        out_shape=(
            jax.ShapeDtypeStruct((ROWS, D), F32),
            jax.ShapeDtypeStruct((ROWS, D), BF),
            jax.ShapeDtypeStruct((D, D), BF),
            jax.ShapeDtypeStruct((1, D), F32),
        ),
        in_specs=[pl.BlockSpec(memory_space=pltpu.SMEM)] + [vm] * 5 + [any_spec()] * (1 + len(arrays)),
        out_specs=(vm,) * 4,
        scratch_shapes=[
            pltpu.VMEM((D, D), BF),
            pltpu.VMEM((ROWS, D), BF),
            pltpu.SemaphoreType.DMA((1,)),
        ],
    )(meta, x2, dn2, og, vp, mixed, own, *arrays)


def attention_back_kernel(q, k, v, do, lse_ref, cos, sin, pq, pk, pv, dk, dv):
    masks = tile_masks()

    def one_pair(p, carry):
        lanes = pl.ds(pl.multiple_of(p * PAIR, PAIR), PAIR)
        dk[...] = jnp.zeros_like(dk)
        dv[...] = jnp.zeros_like(dv)
        for noised in (True, False):
            for t in range(SEQ // TILE):
                row = (0 if noised else SEQ) + TILE * t
                qs = head_split(q[pl.ds(row, TILE), lanes])
                ds = head_split(do[pl.ds(row, TILE), lanes])
                lse = jnp.concatenate(
                    [lse_ref[p, 0:1, row : row + TILE], lse_ref[p, 1:2, row : row + TILE]], axis=1
                )
                parts = key_parts(noised, t, masks)
                probs = [jnp.exp(s - lse) for s in masked_scores(k, lanes, parts, qs)]
                prods = []
                for (start, count, _), e in zip(parts, probs):
                    prods.append(e * mm(v[pl.ds(start, count), lanes], ds, NT))
                    dv[start : start + count, :] += mm(e.astype(BF), ds)
                dot = total_of([jnp.sum(x, axis=0, keepdims=True) for x in prods])
                dq = None
                for (start, count, _), e, x in zip(parts, probs, prods):
                    g = (x - e * dot).astype(BF)
                    dk[start : start + count, :] += mm(g, qs)
                    one = mm(k[pl.ds(start, count), lanes], g, TN)
                    dq = one if dq is None else dq + one
                dq = head_join(dq).T * 0.125
                at = TILE * t
                turn = dq * cos[at : at + TILE, :] - half_swap(dq) * sin[at : at + TILE, :]
                pq[pl.ds(row, TILE), lanes] = turn.astype(BF)
        for half in range(2):
            rows = slice(half * SEQ, (half + 1) * SEQ)
            z = dk[rows, :]
            pk[rows, lanes] = (z * cos[...] - half_swap(z) * sin[...]).astype(BF)
            pv[rows, lanes] = dv[rows, :].astype(BF)
        return carry

    lax.fori_loop(0, NPAIR, one_pair, 0)


def run_attention_back(q, k, v, do, lse, cos, sin):
    vm = pl.BlockSpec(memory_space=pltpu.VMEM)
    sq = jax.ShapeDtypeStruct((ROWS, D), BF)
    return pl.pallas_call(
        attention_back_kernel,
        name="attention_back",
        out_shape=(sq, sq, sq),
        in_specs=[vm] * 7,
        out_specs=(vm,) * 3,
        scratch_shapes=[pltpu.VMEM((ROWS, PAIR), F32), pltpu.VMEM((ROWS, PAIR), F32)],
    )(q, k, v, do, lse, cos, sin)


def qkv_grad_kernel(plans, nwide, meta, n1, pq, pk, pv, gwo, *refs):
    outs = (refs[0:2], refs[2:4])
    res, sems = refs[4:]
    start_scatter(gwo, *outs[1], 1, plans[1], nwide, meta, sems.at[3])
    for i, x in enumerate((pq, pk, pv)):
        res[i] = mm(x[...], n1[...], TN).astype(BF)
        start_scatter(
            res.at[i], *outs[i // 2], i % 2, plans[i // 2], nwide, meta, sems.at[i]
        )
    for i in range(3):
        wait_block(res.at[i], sems.at[i])
    wait_block(gwo, sems.at[3])


def run_qkv_grad(meta, n1, pq, pk, pv, gwo, plans, nwide):
    vm = pl.BlockSpec(memory_space=pltpu.VMEM)
    return pl.pallas_call(
        partial(qkv_grad_kernel, plans, nwide),
        name="qkv_grad",
        out_shape=(scatter_shape(nwide, 2),) * 4,
        in_specs=[pl.BlockSpec(memory_space=pltpu.SMEM)] + [vm] * 5,
        out_specs=(any_spec(),) * 4,
        scratch_shapes=[pltpu.VMEM((3, D, D), BF), pltpu.SemaphoreType.DMA((4,))],
    )(meta, n1, pq, pk, pv, gwo)


def input_grad_kernel(shapes, meta, tok, maskc, vp, dx2, pq, pk, pv, own, *refs):
    nw = sum(n for n, _ in shapes)
    first = split_refs(shapes, refs)
    in_ref, ge_ref, gg_ref = refs[nw : nw + 3]
    wbuf, sems = refs[nw + 3 :]
    for b in range(3):
        start_block(meta, b, own, first, wbuf.at[b], sems.at[b])
    for b in range(3):
        wait_block(wbuf.at[b], sems.at[b])
    gg = jnp.zeros((1, D), F32)
    kept = None
    for half in range(2):
        rows = slice(half * SEQ, (half + 1) * SEQ)
        dn = total_of([mm(x[rows, :], wbuf[b], NT) for b, x in enumerate((pq, pk, pv))])
        cen, r = norm_stats(input_rows(tok, maskc, vp, half))
        zh = cen * r
        gg = gg + jnp.sum(dn * zh, axis=0, keepdims=True)
        dx = dx2[rows, :] + norm_back(zh, r, dn * vp[1:2, :])
        if half == 0:
            hit = maskc[...] == 1
            ge_ref[...] = jnp.sum(jnp.where(hit, dx, 0.0), axis=0, keepdims=True)
            kept = jnp.where(hit, 0.0, dx)
        else:
            in_ref[...] = (dx + kept).astype(BF)
    gg_ref[...] = gg


def run_input_grad(meta, tok, maskc, vp, dx2, pq, pk, pv, own, first):
    vm = pl.BlockSpec(memory_space=pltpu.VMEM)
    arrays = group_arrays(first)
    return pl.pallas_call(
        partial(input_grad_kernel, group_shapes(first)),
        name="input_grad",
        out_shape=(
            jax.ShapeDtypeStruct((SEQ, D), BF),
            jax.ShapeDtypeStruct((1, D), F32),
            jax.ShapeDtypeStruct((1, D), F32),
        ),
        in_specs=[pl.BlockSpec(memory_space=pltpu.SMEM)] + [vm] * 7 + [any_spec()] * (1 + len(arrays)),
        out_specs=(vm,) * 3,
        scratch_shapes=[pltpu.VMEM((3, D, D), BF), pltpu.SemaphoreType.DMA((3,))],
    )(meta, tok, maskc, vp, dx2, pq, pk, pv, own, *arrays)


def send_kernel(scalars, direct, tree, *outs):
    outs[0][...] = direct[...].astype(BF)
    if len(outs) > 1:
        outs[1][...] = tree[...].astype(BF)


def run_send(scalars, weights, nwide, at, count, tree_at, tree_count):
    rows = D // nwide
    outs = [jax.ShapeDtypeStruct((count, D // 2, D), BF)]
    specs = [pl.BlockSpec((1, D // 2, D), lambda s, sc: (s, 0, 0))]
    if tree_count:
        outs.append(jax.ShapeDtypeStruct((tree_count, rows, D), BF))
        specs.append(
            pl.BlockSpec((1, rows, D), lambda s, sc: (jnp.minimum(s, tree_count - 1), 0, 0))
        )
    return pl.pallas_call(
        send_kernel,
        name="send_weights",
        grid_spec=pltpu.PrefetchScalarGridSpec(
            num_scalar_prefetch=1,
            grid=(count,),
            in_specs=[
                pl.BlockSpec((1, D // 2, D), lambda s, sc: (sc[2 + at + s], sc[1], 0)),
                pl.BlockSpec(
                    (1, rows, D),
                    lambda s, sc: (sc[2 + tree_at + jnp.minimum(s, max(tree_count, 1) - 1)], sc[0], 0),
                ),
            ],
            out_specs=tuple(specs),
        ),
        out_shape=tuple(outs),
    )(scalars, weights, weights)


def turn_kernel(count, sizes, shapes, meta, items, slots, *refs):
    grads = refs[: len(sizes)]
    refs = refs[len(sizes) :]
    nw = sum(n for n, _ in shapes)
    (left,) = split_refs(shapes, refs)
    out = refs[nw]
    lbuf, gbuf, lsem, gsem = refs[nw + 1 :]
    for s in range(count):
        item = items[s]
        if len(grads) == 1:
            pltpu.make_async_copy(grads[0].at[item], gbuf.at[s], gsem.at[s]).start()
        else:

            @pl.when(item < sizes[0])
            def _():
                pltpu.make_async_copy(grads[0].at[item], gbuf.at[s], gsem.at[s]).start()

            @pl.when(item >= sizes[0])
            def _():
                pltpu.make_async_copy(
                    grads[1].at[item - sizes[0]], gbuf.at[s], gsem.at[s]
                ).start()

        start_slices(left, slots[s], lbuf.at[s], lsem.at[s], meta[0])
    parts = []
    for s in range(count):
        wait_block(gbuf.at[s], gsem.at[s])
        wait_block(lbuf.at[s], lsem.at[s])
        parts.append(mm(lbuf[s], gbuf[s], NT))
    out[...] = jnp.concatenate(parts, axis=1).astype(BF)


def run_turn(meta, items, slots, grads, left):
    count = items.shape[0]
    rows = grads[0].shape[1]
    sizes = tuple(g.shape[0] for g in grads)
    smem = pl.BlockSpec(memory_space=pltpu.SMEM)
    return pl.pallas_call(
        partial(turn_kernel, count, sizes, group_shapes([left])),
        name="gradient_turn",
        out_shape=jax.ShapeDtypeStruct((D, count * rows), BF),
        in_specs=[smem] * 3 + [any_spec()] * (len(grads) + len(left.arrays)),
        out_specs=pl.BlockSpec(memory_space=pltpu.VMEM),
        scratch_shapes=[
            pltpu.VMEM((count, D, D), BF),
            pltpu.VMEM((count, rows, D), BF),
            pltpu.SemaphoreType.DMA((count,)),
            pltpu.SemaphoreType.DMA((count,)),
        ],
    )(meta, items, slots, *grads, *left.arrays)


def adam_kernel(count, chained, slots, live, grads, first, second, right, *refs):
    nf, ns, back, full = refs[2 if chained else 0 :]
    s = pl.program_id(0)
    rows = first.shape[1]

    @pl.when(s == 0)
    def _():
        for k in range(count):
            for src in range(D // rows):
                at = slice(src * rows, (src + 1) * rows)
                full[k, :, at] = grads[at, k * rows : (k + 1) * rows].astype(F32)

    @pl.when(live[s] == 1)
    def _():
        basis = right[0].astype(BF)
        turned = mm(full[s].astype(BF), basis)
        one = BETA * first[0] + (1.0 - BETA) * turned
        two = BETA * second[0] + (1.0 - BETA) * turned * turned
        nf[0] = one
        ns[0] = two
        step = one / (jnp.sqrt(two) + EPS_ADAM)
        back[0] = mm(step.astype(BF), basis, NT).astype(BF)

    @pl.when(live[s] == 0)
    def _():
        nf[...] = jnp.zeros_like(nf)
        ns[...] = jnp.zeros_like(ns)
        back[...] = jnp.zeros_like(back)


def run_adam(slots, live, grads, first, second, right, earlier):
    count = slots.shape[0]
    rows = first.shape[1]
    state = pl.BlockSpec((1, rows, D), lambda s, slots, live: (slots[s], 0, 0))
    return pl.pallas_call(
        partial(adam_kernel, count, bool(earlier)),
        name="adam_step",
        grid_spec=pltpu.PrefetchScalarGridSpec(
            num_scalar_prefetch=2,
            grid=(count,),
            in_specs=[
                pl.BlockSpec(grads.shape, lambda s, *_: (0, 0)),
                state,
                state,
                pl.BlockSpec((1, D, D), lambda s, slots, live: (slots[s], 0, 0)),
            ]
            + [any_spec()] * len(earlier),
            out_specs=(state, state, pl.BlockSpec((1, rows, D), lambda s, *_: (s, 0, 0))),
            scratch_shapes=[pltpu.VMEM((count, rows, D), F32)],
        ),
        out_shape=(
            jax.ShapeDtypeStruct(first.shape, F32),
            jax.ShapeDtypeStruct(first.shape, F32),
            jax.ShapeDtypeStruct((count, rows, D), BF),
        ),
        input_output_aliases={6: 0, 7: 1} if earlier else {},
    )(slots, live, grads, first, second, right, *earlier)


def update_kernel(shapes, half, chained, slots, live, meta, weights, *refs):
    nw = sum(n for n, _ in shapes)
    back_a, back_b, left = split_refs(shapes, refs)
    out, lbuf, bbuf, lsem, bsem = refs[nw + (1 if chained else 0) :]
    s = pl.program_id(0)
    count = pl.num_programs(0)
    me = meta[0]
    slot = s % 2

    def begin(item, where):
        @pl.when(live[item] == 1)
        def _():
            @pl.when(item < half)
            def _():
                start_slices(back_a, item, bbuf.at[where], bsem.at[where], me)

            @pl.when(item >= half)
            def _():
                start_slices(back_b, item - half, bbuf.at[where], bsem.at[where], me)

            start_slices(left, slots[item], lbuf.at[where], lsem.at[where], me)

    @pl.when(s == 0)
    def _():
        begin(0, 0)

    @pl.when(s + 1 < count)
    def _():
        begin(s + 1, 1 - slot)

    @pl.when(live[s] == 1)
    def _():
        wait_block(lbuf.at[slot], lsem.at[slot])
        wait_block(bbuf.at[slot], bsem.at[slot])
        out[0] = weights[0] - RATE_MATRIX * mm(lbuf[slot], bbuf[slot], TN)

    @pl.when(live[s] == 0)
    def _():
        out[...] = jnp.zeros_like(out)


def run_update(slots, live, meta, weights, backs, half, left, earlier):
    groups = backs + [left]
    arrays = group_arrays(groups)
    whole = pl.BlockSpec((1, D, D), lambda s, slots, *_: (slots[s], 0, 0))
    return pl.pallas_call(
        partial(update_kernel, group_shapes(groups), half, bool(earlier)),
        name="weight_update",
        grid_spec=pltpu.PrefetchScalarGridSpec(
            num_scalar_prefetch=3,
            grid=(slots.shape[0],),
            in_specs=[whole] + [any_spec()] * (len(arrays) + len(earlier)),
            out_specs=whole,
            scratch_shapes=[
                pltpu.VMEM((2, D, D), BF),
                pltpu.VMEM((2, D, D), BF),
                pltpu.SemaphoreType.DMA((2,)),
                pltpu.SemaphoreType.DMA((2,)),
            ],
        ),
        out_shape=jax.ShapeDtypeStruct(weights.shape, F32),
        input_output_aliases={4 + len(arrays): 0} if earlier else {},
    )(slots, live, meta, weights, *arrays, *earlier)


def rotary_tables():
    half_size = D // HEADS // 2
    position_col = jnp.arange(SEQ, dtype=jnp.int32).astype(F32)
    frequency = jnp.exp(
        jnp.arange(half_size, dtype=F32) * (-2.0 * math.log(10000.0) / (2 * half_size))
    )
    angles = position_col[:, None] * frequency[None, :]
    cosine = jnp.cos(angles)
    sine = jnp.sin(angles)
    return (
        jnp.concatenate([cosine, cosine, cosine, cosine], axis=1),
        jnp.concatenate([-sine, sine, -sine, sine], axis=1),
    )


def on_device(nwide, nnarrow, *args):
    return whole_step(nwide, nnarrow, *args)


def whole_step(
    nwide,
    nnarrow,
    tokens,
    masked,
    out_grad,
    slot_block,
    weights,
    vectors,
    vec_first,
    vec_second,
    mom_first,
    mom_second,
    basis_left,
    basis_right,
):
    sd = weights.shape[0]
    slots = sd * nnarrow
    w = lax.axis_index("wide").astype(jnp.int32)
    n = lax.axis_index("narrow").astype(jnp.int32)
    top = nnarrow // 2
    nbit = n // top
    far_order = far_bits(nwide)
    left_order = far_order[:1] + far_order[-2:-1] + far_order[1:-2] + far_order[-1:]
    inner = [("wide", nwide, bit) for bit in far_order[-2::-1]]
    split = [("narrow", nnarrow, top)]
    near_x = tuple(split + inner)
    near_y = tuple(inner[:1] + split + inner[1:])

    ids = jnp.arange(slots, dtype=jnp.int32)
    hits = slot_block[None, :] == jnp.arange(NBLK, dtype=jnp.int32)[:, None]
    block_slot = jnp.sum(jnp.where(hits, ids[None, :], 0), axis=1)
    earlier = (
        (slot_block[None, :] < slot_block[:, None])
        | ((slot_block[None, :] == slot_block[:, None]) & (ids[None, :] < ids[:, None]))
    ) & (ids[None, :] // sd == ids[:, None] // sd)
    slot_rank = jnp.sum(earlier.astype(jnp.int32), axis=1)
    block_rank = jnp.sum(jnp.where(hits, slot_rank[None, :], 0), axis=1)
    own_blocks = lax.dynamic_slice_in_dim(slot_block, n * sd, sd)
    own_rank = lax.dynamic_slice_in_dim(slot_rank, n * sd, sd)
    at_rank = own_rank[None, :] == jnp.arange(sd, dtype=jnp.int32)[:, None]
    sorted_slots = jnp.sum(
        jnp.where(at_rank, jnp.arange(sd, dtype=jnp.int32)[None, :], 0), axis=1
    )
    sorted_blocks = jnp.sum(jnp.where(at_rank, own_blocks[None, :], 0), axis=1)
    sorted_live = (sorted_blocks < NBLK).astype(jnp.int32)

    scalars = jnp.concatenate([w[None], (w & 1)[None], sorted_slots]).astype(jnp.int32)
    c1 = min(4, sd)
    d1 = c1 // 2
    pieces = [("d1", 0, d1, True), ("t1", d1, c1 - d1, False)]
    if sd > c1:
        mid = (sd - c1) // 2
        pieces += [("d2", c1, mid, True), ("t2", c1 + mid, sd - c1 - mid, False)]

    def spread(x, direct):
        got = narrow_parts(x, nnarrow)[1:]
        got = got[0] if len(got) == 1 else jnp.concatenate(got, axis=0)
        if direct:
            return wide_group(got, nwide, [1], 0)
        return wide_group(got, nwide, far_order, len(far_order) - 2)

    direct, tree = run_send(scalars, weights, nwide, 0, d1, d1, c1 - d1)
    early_tree = spread(tree, False)
    early_direct = spread(direct, True)
    first = [early_direct, early_tree]
    groups = list(first)
    if sd > c1:
        direct, tree = run_send(scalars, weights, nwide, c1, mid, c1 + mid, sd - c1 - mid)
        groups += [spread(direct, True), spread(tree, False)]
    own = weights.astype(BF)

    far = n ^ (block_slot // sd)
    source = jnp.zeros((NBLK,), jnp.int32)
    index = block_slot % sd
    for k, (_, at, count, _) in enumerate(pieces):
        here = (far > 0) & (block_rank >= at) & (block_rank < at + count)
        source = jnp.where(here, k + 1, source)
        index = jnp.where(here, (far - 1) * count + block_rank - at, index)
    meta = jnp.concatenate([w[None], nbit[None], source, index]).astype(jnp.int32)

    vec_rel = jnp.stack(narrow_parts(vectors.astype(BF), nnarrow))
    vec_all = vec_rel[n ^ jnp.arange(nnarrow, dtype=jnp.int32)].reshape(8, D).astype(F32)

    left = basis_left.transpose(0, 2, 1).astype(BF)
    left = wide_group(left, nwide, left_order, len(left_order) - 2)

    cos, sin = rotary_tables()
    tok = tokens[0]
    maskc = masked[0][:, None]
    og = out_grad[0]

    q, k, v, n1, mixed, lse, x2, n2 = run_forward(meta, tok, maskc, vec_all, cos, sin, own, first)
    layer_out, up_keep, up_send, down_keep, down_send, dn2, gbias = run_ffn(
        meta, n2, og, x2, vec_all, own, groups, (near_y, near_x), nwide
    )

    def reduced(keep, send, steps):
        total = scatter_sum(keep, send, nwide, steps)
        rest = far_bits(nnarrow)[1:]
        total = butterfly_sum(total, "narrow", nnarrow, rest, BF).astype(BF)
        return [total, xor_permute(total, "narrow", nnarrow, top)]

    gdown = reduced(down_keep, down_send, near_x)
    gup = reduced(up_keep, up_send, near_y)
    dx2, do, gwo, gg2 = run_resid(meta, x2, dn2, og, vec_all, mixed, own, first)
    pq, pk, pv = run_attention_back(q, k, v, do, lse, cos, sin)
    qk_keep, qk_send, vo_keep, vo_send = run_qkv_grad(
        meta, n1, pq, pk, pv, gwo, (near_x, near_y), nwide
    )
    gqk = reduced(qk_keep, qk_send, near_x)
    gvo = reduced(vo_keep, vo_send, near_y)
    in_grad, ge, gg1 = run_input_grad(
        meta, tok, maskc, vec_all, dx2, pq, pk, pv, own, first
    )

    chunks = [(0, c1, 0)]
    if sd > c1:
        chunks = [(c1, sd, 4)] + chunks
    state = ()
    fresh = ()
    ffn_grads = jnp.concatenate(gup + gdown, axis=0)
    att_grads = jnp.concatenate(gqk + gvo, axis=0)
    for lo, hi, base in chunks:
        grads = [ffn_grads] if base else [att_grads, ffn_grads]
        block = jnp.clip(sorted_blocks[lo:hi], base, NBLK - 1)
        width = jnp.where(block < 4, 1, 2)
        start = jnp.where(block < 4, block // 2 * 2, block // 4 * 4)
        items = start - base + ((block & 1) ^ nbit) * width + (block - start) // 2
        held = sorted_slots[lo:hi]
        live = sorted_live[lo:hi]
        turned = run_turn(meta, items, held, grads, left)
        turned = lax.all_to_all(turned, "wide", 0, 0, tiled=True)
        *state, back = run_adam(
            held, live, turned, mom_first, mom_second, basis_right, state
        )
        half = (hi - lo + 1) // 2
        merge = len(far_order) - 2
        backs = [
            wide_group(back[:half], nwide, far_order, merge),
            wide_group(back[half:], nwide, left_order, merge),
        ]
        fresh = (run_update(held, live, meta, weights, backs, half, left, fresh),)
    new_first, new_second = state
    new_weights = fresh[0]

    vec_grad = jnp.concatenate([ge, gg1, gg2, gbias[: FFB + 1]], axis=0)
    vec_grad = butterfly_sum(vec_grad, "narrow", nnarrow, far_bits(nnarrow))
    vec_grad = butterfly_sum(vec_grad, "wide", nwide, far_order[:-1])
    vec_grad = butterfly_sum(vec_grad, "wide", nwide, far_order[-1:])
    vec_owned = lax.dynamic_slice_in_dim(
        vec_grad.reshape(nnarrow, vectors.shape[0]), n, 1, axis=0
    )[0]
    vec_mean = BETA * vec_first + (1.0 - BETA) * vec_owned
    vec_square = BETA * vec_second + (1.0 - BETA) * vec_owned * vec_owned
    vec_new = vectors - RATE_VECTOR * vec_mean / (jnp.sqrt(vec_square) + EPS_ADAM)
    return (
        layer_out[None],
        in_grad[None],
        new_weights,
        new_first,
        new_second,
        vec_new,
        vec_mean,
        vec_square,
    )


def solution(mesh):
    return jax.shard_map(
        partial(on_device, mesh.shape["wide"], mesh.shape["narrow"]),
        mesh=mesh,
        in_specs=(
            P(("wide", "narrow"), None, None),
            P(("wide", "narrow"), None),
            P(("wide", "narrow"), None, None),
            P(),
            P("narrow", None, None),
            P("narrow"),
            P("narrow"),
            P("narrow"),
            P("narrow", "wide", None),
            P("narrow", "wide", None),
            P("narrow", None, "wide"),
            P("narrow", None, None),
        ),
        out_specs=(
            P(("wide", "narrow"), None, None),
            P(("wide", "narrow"), None, None),
            P("narrow", None, None),
            P("narrow", "wide", None),
            P("narrow", "wide", None),
            P("narrow"),
            P("narrow"),
            P("narrow"),
        ),
        check_vma=False,
    )
```

```python
from functools import partial
import math
from typing import NamedTuple

import jax
import jax.numpy as jnp
from jax import lax
from jax.experimental import pallas as pl
from jax.experimental.pallas import tpu as pltpu
from jax.sharding import PartitionSpec as P


D = 768
HEADS = 12
FF = 3072
BLK = 16
SEQ = 384
NBLK = 12
ROWS = 2 * SEQ
FFB = FF // D
PAIR = 128
NPAIR = D // PAIR
TILE = 128
CHUNK = 256

EPS_NORM = 1e-05
EPS_ADAM = 1e-08
RATE_MATRIX = 0.05
RATE_VECTOR = 0.3
BETA = 0.5
MASK_FILL = -1e30
GELU_A = math.sqrt(2.0 / math.pi)
GELU_B = 0.044715

BF = jnp.bfloat16
F32 = jnp.float32


NT = (((1,), (1,)), ((), ()))
TN = (((0,), (0,)), ((), ()))
NN = (((1,), (0,)), ((), ()))


def mm(a, b, dims=NN):
    return lax.dot_general(a, b, dims, preferred_element_type=F32)


def any_spec():
    return pl.BlockSpec(memory_space=pl.ANY)


class Group(NamedTuple):
    arrays: tuple
    where: tuple


def xor_permute(x, axis, size, mask):
    return lax.ppermute(x, axis, [(i, i ^ mask) for i in range(size)])


def far_bits(size):
    bits = []
    bit = size // 2
    while bit:
        bits.append(bit)
        bit //= 2
    return bits


def narrow_parts(x, size):
    have = {0: x}
    for bit in far_bits(size):
        fresh = {r | bit: xor_permute(have[r], "narrow", size, bit) for r in have}
        have.update(fresh)
    return [have[r] for r in range(size)]


def wide_group(x, size, order, merge):
    bufs = [(x[None], [0])]
    for i, bit in enumerate(order):
        fresh = [(xor_permute(a, "wide", size, bit), [r | bit for r in rels]) for a, rels in bufs]
        bufs = bufs + fresh
        if i < merge:
            bufs = [(jnp.concatenate([a for a, _ in bufs], axis=0), sum((r for _, r in bufs), []))]
    where = [None] * (2 ** len(order))
    for i, (_, rels) in enumerate(bufs):
        for j, r in enumerate(rels):
            where[r] = (i, j)
    return Group(tuple(a for a, _ in bufs), tuple(where))


def scatter_sum(keep, send, nwide, steps):
    parts = [keep, xor_permute(send, "wide", nwide, 1)]
    cur = keep.shape[0]
    for axis, size, bit in steps:
        half = cur // 2
        total = total_of([p[half:cur].astype(F32) for p in parts])
        got = xor_permute(total.astype(BF), axis, size, bit)
        parts = [p[:half] for p in parts] + [got]
        cur = half
    return total_of([p[0].astype(F32) for p in parts])


def butterfly_sum(x, axis, size, order, low=None):
    for bit in order:
        sent = x if low is None else x.astype(low)
        x = x + xor_permute(sent, axis, size, bit).astype(x.dtype)
    return x


def split_refs(groups, refs):
    out = []
    at = 0
    for arrays, where in groups:
        out.append((refs[at : at + arrays], where))
        at += arrays
    return out


def group_shapes(groups):
    return tuple((len(g.arrays), g.where) for g in groups)


def group_arrays(groups):
    return [a for g in groups for a in g.arrays]


def start_slices(group, index, dst, sem, me):
    refs, where = group
    count = len(where)
    rows = D // count
    base = me & (count - 1)
    for r, (i, j) in enumerate(where):
        at = pl.multiple_of((base ^ r) * rows, rows)
        pltpu.make_async_copy(refs[i].at[j, index], dst.at[pl.ds(at, rows)], sem).start()


def start_block(meta, block, own, groups, dst, sem):
    me = meta[0]
    source = meta[2 + block]
    index = meta[2 + NBLK + block]

    @pl.when(source == 0)
    def _():
        pltpu.make_async_copy(own.at[index], dst, sem).start()

    for k, group in enumerate(groups):

        @pl.when(source == k + 1)
        def _():
            start_slices(group, index, dst, sem, me)


def start_scatter(src, keep, send, item, steps, nwide, meta, sem):
    me = meta[0]
    rows = D // nwide
    side = (item & 1) ^ meta[1]
    for r in range(nwide):
        at = 0
        for axis, _, bit in steps:
            at = at * 2 + (side if axis == "narrow" else (1 if r & bit else 0))
        dst = send if r & 1 else keep
        row = pl.multiple_of((me ^ r) * rows, rows)
        pltpu.make_async_copy(src.at[pl.ds(row, rows)], dst.at[at, item // 2], sem).start()


def wait_block(dst, sem):
    pltpu.make_async_copy(dst, dst, sem).wait()


def norm_stats(z):
    mean = jnp.mean(z, axis=-1, keepdims=True)
    cen = z - mean
    var = jnp.mean(cen * cen, axis=-1, keepdims=True)
    return cen, lax.rsqrt(var + EPS_NORM)


def norm_back(zh, r, dz):
    return r * (
        dz
        - jnp.mean(dz, axis=-1, keepdims=True)
        - zh * jnp.mean(dz * zh, axis=-1, keepdims=True)
    )


def half_swap(z):
    lane = lax.broadcasted_iota(jnp.int32, z.shape, 1) % 64
    return jnp.where(lane < 32, pltpu.roll(z, PAIR - 32, 1), pltpu.roll(z, 32, 1))


def tile_masks():
    key = lax.broadcasted_iota(jnp.int32, (TILE, 2 * TILE), 0) // BLK
    qry = lax.broadcasted_iota(jnp.int32, (TILE, 2 * TILE), 1) % TILE // BLK
    return key == qry, key < qry, key <= qry


def head_split(x):
    lane = lax.broadcasted_iota(jnp.int32, x.shape, 1)
    zero = jnp.zeros_like(x)
    return jnp.concatenate([jnp.where(lane < 64, x, zero), jnp.where(lane < 64, zero, x)], axis=0)


def head_join(xt):
    row = lax.broadcasted_iota(jnp.int32, (PAIR, TILE), 0)
    return jnp.where(row < 64, xt[:, :TILE], xt[:, TILE:])


def key_parts(noised, t, masks):
    same, before, upto = masks
    parts = []
    if t > 0:
        parts.append((SEQ, TILE * t, None))
    parts.append((SEQ + TILE * t, TILE, before if noised else upto))
    if noised:
        parts.append((TILE * t, TILE, same))
    return parts


def masked_scores(k_ref, lanes, parts, qs):
    out = []
    for start, count, mask in parts:
        s = mm(k_ref[pl.ds(start, count), lanes], qs, NT)
        out.append(s if mask is None else jnp.where(mask, s, MASK_FILL))
    return out


def total_of(items):
    total = items[0]
    for x in items[1:]:
        total = total + x
    return total


def input_rows(tok_ref, mask_ref, vp_ref, half):
    tok = tok_ref[...].astype(F32)
    if half == 1:
        return tok
    return jnp.where(mask_ref[...] == 1, vp_ref[0:1, :], tok)


def start_blocks(meta, count, own, groups, dst, sems):
    def begin(b, carry):
        start_block(meta, b, own, groups, dst.at[b], sems.at[b])
        return carry

    lax.fori_loop(0, count, begin, 0)


def qkv_kernel(shapes, meta, tok, maskc, vp, cos, sin, own, *refs):
    nw = sum(n for n, _ in shapes)
    first = split_refs(shapes, refs)
    q_ref, k_ref, v_ref, n1_ref, wbuf, sems = refs[nw:]
    start_blocks(meta, 3, own, first, wbuf, sems)
    for half in range(2):
        cen, r = norm_stats(input_rows(tok, maskc, vp, half))
        n1_ref[half * SEQ : (half + 1) * SEQ, :] = (cen * r * vp[1:2, :]).astype(BF)
    for b, out in enumerate((q_ref, k_ref, v_ref)):
        wait_block(wbuf.at[b], sems.at[b])
        for half in range(2):
            rows = slice(half * SEQ, (half + 1) * SEQ)
            for c in range(D // CHUNK):
                z = mm(n1_ref[rows, :], wbuf[b, :, c * CHUNK : (c + 1) * CHUNK])
                for s in range(CHUNK // PAIR):
                    piece = z[:, s * PAIR : (s + 1) * PAIR]
                    if b < 2:
                        piece = piece * cos[...] + half_swap(piece) * sin[...]
                    if b == 0:
                        piece = piece * 0.125
                    at = c * CHUNK + s * PAIR
                    out[rows, at : at + PAIR] = piece.astype(BF)


def run_qkv(meta, tok, maskc, vp, cos, sin, own, first):
    vm = pl.BlockSpec(memory_space=pltpu.VMEM)
    arrays = group_arrays(first)
    return pl.pallas_call(
        partial(qkv_kernel, group_shapes(first)),
        name="project_qkv",
        out_shape=(jax.ShapeDtypeStruct((ROWS, D), BF),) * 4,
        in_specs=[pl.BlockSpec(memory_space=pltpu.SMEM)] + [vm] * 5 + [any_spec()] * (1 + len(arrays)),
        out_specs=(vm,) * 4,
        scratch_shapes=[pltpu.VMEM((3, D, D), BF), pltpu.SemaphoreType.DMA((3,))],
    )(meta, tok, maskc, vp, cos, sin, own, *arrays)


def forward_kernel(shapes, meta, tok, maskc, vp, q_ref, k_ref, v_ref, own, *refs):
    nw = sum(n for n, _ in shapes)
    first = split_refs(shapes, refs)
    o_ref, lse_ref, x2_ref, n2_ref, wbuf, sems = refs[nw:]
    start_block(meta, 3, own, first, wbuf, sems.at[0])
    masks = tile_masks()

    def one_pair(p, carry):
        lanes = pl.ds(pl.multiple_of(p * PAIR, PAIR), PAIR)
        for noised in (True, False):
            for t in range(SEQ // TILE):
                row = (0 if noised else SEQ) + TILE * t
                qs = head_split(q_ref[pl.ds(row, TILE), lanes])
                parts = key_parts(noised, t, masks)
                scores = masked_scores(k_ref, lanes, parts, qs)
                tops = [jnp.max(s, axis=0, keepdims=True) for s in scores]
                top = tops[0]
                for x in tops[1:]:
                    top = jnp.maximum(top, x)
                expo = [jnp.exp(s - top) for s in scores]
                total = total_of([jnp.sum(e, axis=0, keepdims=True) for e in expo])
                mixed = total_of(
                    [
                        mm(v_ref[pl.ds(start, count), lanes], e.astype(BF), TN)
                        for (start, count, _), e in zip(parts, expo)
                    ]
                )
                mixed = mixed * (1.0 / total)
                o_ref[pl.ds(row, TILE), lanes] = head_join(mixed).T.astype(BF)
                lse = top + jnp.log(total)
                lse_ref[p, 0:1, row : row + TILE] = lse[:, :TILE]
                lse_ref[p, 1:2, row : row + TILE] = lse[:, TILE:]
        return carry

    lax.fori_loop(0, NPAIR, one_pair, 0)
    wait_block(wbuf, sems.at[0])
    for half in range(2):
        rows = slice(half * SEQ, (half + 1) * SEQ)
        x2 = input_rows(tok, maskc, vp, half) + mm(o_ref[rows, :], wbuf[...])
        x2_ref[rows, :] = x2
        cen, r = norm_stats(x2)
        n2_ref[rows, :] = (cen * r * vp[2:3, :]).astype(BF)


def run_forward(meta, tok, maskc, vp, q, k, v, own, first):
    vm = pl.BlockSpec(memory_space=pltpu.VMEM)
    sq = jax.ShapeDtypeStruct((ROWS, D), BF)
    arrays = group_arrays(first)
    return pl.pallas_call(
        partial(forward_kernel, group_shapes(first)),
        name="forward_attention",
        out_shape=(
            sq,
            jax.ShapeDtypeStruct((NPAIR, 2, ROWS), F32),
            jax.ShapeDtypeStruct((ROWS, D), F32),
            sq,
        ),
        in_specs=[pl.BlockSpec(memory_space=pltpu.SMEM)] + [vm] * 6 + [any_spec()] * (1 + len(arrays)),
        out_specs=(vm,) * 4,
        scratch_shapes=[pltpu.VMEM((D, D), BF), pltpu.SemaphoreType.DMA((1,))],
    )(meta, tok, maskc, vp, q, k, v, own, *arrays)


def ffn_kernel(shapes, plans, nwide, meta, n2, og, x2, vp, own, *refs):
    nw = sum(n for n, _ in shapes)
    groups = split_refs(shapes, refs)
    layer_ref, up_keep, up_send, down_keep, down_send, dn2_ref, gbias_ref = refs[nw : nw + 7]
    wup, wdown, yacc, act, dhid, gup, gdown, sems, gsem = refs[nw + 7 :]
    f = pl.program_id(0)
    slot = f % 2

    @pl.when(f == 0)
    def _():
        def begin(b, carry):
            start_block(meta, 4 + b, own, groups, wup.at[b], sems.at[b])
            start_block(meta, 8 + b, own, groups, wdown.at[b], sems.at[4 + b])
            return carry

        lax.fori_loop(0, FFB, begin, 0)
        yacc[...] = jnp.zeros_like(yacc)
        dn2_ref[...] = jnp.zeros_like(dn2_ref)
        gbias_ref[FFB : FFB + 1, :] = jnp.sum(og[...].astype(F32), axis=0, keepdims=True)

    @pl.when(f > 1)
    def _():
        wait_block(gup.at[slot], gsem.at[slot])
        wait_block(gdown.at[slot], gsem.at[2 + slot])

    wait_block(wup.at[f], sems.at[f])
    wait_block(wdown.at[f], sems.at[4 + f])
    bias = vp[pl.ds(3 + f, 1), :]
    gb = jnp.zeros((1, D), F32)
    for c in range(ROWS // CHUNK):
        rows = slice(c * CHUNK, (c + 1) * CHUNK)
        h = mm(n2[rows, :], wup[f]) + bias
        hh = h * h
        th = jnp.tanh(h * (GELU_A + (GELU_A * GELU_B) * hh))
        lift = 0.5 + 0.5 * th
        slope = lift + (0.5 * h) * (1.0 - th * th) * (GELU_A + (3.0 * GELU_A * GELU_B) * hh)
        act[rows, :] = (h * lift).astype(BF)
        dh = mm(og[rows, :], wdown[f], NT) * slope
        gb = gb + jnp.sum(dh, axis=0, keepdims=True)
        dhid[rows, :] = dh.astype(BF)
        yacc[rows, :] += mm(act[rows, :], wdown[f])
        dn2_ref[rows, :] += mm(dhid[rows, :], wup[f], NT)
    gbias_ref[pl.ds(f, 1), :] = gb
    gdown[slot] = mm(og[...], act[...], TN).astype(BF)
    start_scatter(
        gdown.at[slot], down_keep, down_send, f, plans[1], nwide, meta, gsem.at[2 + slot]
    )
    gup[slot] = mm(dhid[...], n2[...], TN).astype(BF)
    start_scatter(gup.at[slot], up_keep, up_send, f, plans[0], nwide, meta, gsem.at[slot])

    @pl.when(f == FFB - 1)
    def _():
        layer_ref[...] = (x2[...] + yacc[...] + vp[7:8, :]).astype(BF)
        for k in range(2):
            wait_block(gup.at[k], gsem.at[k])
            wait_block(gdown.at[k], gsem.at[2 + k])


def scatter_shape(nwide, count):
    return jax.ShapeDtypeStruct((nwide, count // 2, D // nwide, D), BF)


def run_ffn(meta, n2, og, x2, vp, own, groups, plans, nwide):
    def whole(shape):
        return pl.BlockSpec(shape, lambda f: (0,) * len(shape))

    arrays = group_arrays(groups)
    part = scatter_shape(nwide, FFB)
    return pl.pallas_call(
        partial(ffn_kernel, group_shapes(groups), plans, nwide),
        name="feed_forward",
        grid=(FFB,),
        out_shape=(
            jax.ShapeDtypeStruct((ROWS, D), BF),
            part,
            part,
            part,
            part,
            jax.ShapeDtypeStruct((ROWS, D), F32),
            jax.ShapeDtypeStruct((8, D), F32),
        ),
        in_specs=[
            pl.BlockSpec(memory_space=pltpu.SMEM),
            whole((ROWS, D)),
            whole((ROWS, D)),
            whole((ROWS, D)),
            whole((8, D)),
        ]
        + [any_spec()] * (1 + len(arrays)),
        out_specs=(whole((ROWS, D)),) + (any_spec(),) * 4 + (whole((ROWS, D)), whole((8, D))),
        scratch_shapes=[
            pltpu.VMEM((FFB, D, D), BF),
            pltpu.VMEM((FFB, D, D), BF),
            pltpu.VMEM((ROWS, D), F32),
            pltpu.VMEM((ROWS, D), BF),
            pltpu.VMEM((ROWS, D), BF),
            pltpu.VMEM((2, D, D), BF),
            pltpu.VMEM((2, D, D), BF),
            pltpu.SemaphoreType.DMA((2 * FFB,)),
            pltpu.SemaphoreType.DMA((4,)),
        ],
    )(meta, n2, og, x2, vp, own, *arrays)


def resid_kernel(shapes, meta, x2, dn2, og, vp, o_ref, own, *refs):
    nw = sum(n for n, _ in shapes)
    first = split_refs(shapes, refs)
    dx2_ref, do_ref, gwo_ref, gg_ref = refs[nw : nw + 4]
    wbuf, dlow, sems = refs[nw + 4 :]
    start_block(meta, 3, own, first, wbuf, sems.at[0])
    gg = jnp.zeros((1, D), F32)
    for c in range(ROWS // CHUNK):
        rows = slice(c * CHUNK, (c + 1) * CHUNK)
        cen, r = norm_stats(x2[rows, :])
        zh = cen * r
        dn = dn2[rows, :]
        gg = gg + jnp.sum(dn * zh, axis=0, keepdims=True)
        dx = og[rows, :].astype(F32) + norm_back(zh, r, dn * vp[2:3, :])
        dx2_ref[rows, :] = dx
        dlow[rows, :] = dx.astype(BF)
    gg_ref[...] = gg
    gwo_ref[...] = mm(dlow[...], o_ref[...], TN).astype(BF)
    wait_block(wbuf, sems.at[0])
    do_ref[...] = mm(dlow[...], wbuf[...], NT).astype(BF)


def run_resid(meta, x2, dn2, og, vp, mixed, own, first):
    vm = pl.BlockSpec(memory_space=pltpu.VMEM)
    arrays = group_arrays(first)
    return pl.pallas_call(
        partial(resid_kernel, group_shapes(first)),
        name="residual_back",
        out_shape=(
            jax.ShapeDtypeStruct((ROWS, D), F32),
            jax.ShapeDtypeStruct((ROWS, D), BF),
            jax.ShapeDtypeStruct((D, D), BF),
            jax.ShapeDtypeStruct((1, D), F32),
        ),
        in_specs=[pl.BlockSpec(memory_space=pltpu.SMEM)] + [vm] * 5 + [any_spec()] * (1 + len(arrays)),
        out_specs=(vm,) * 4,
        scratch_shapes=[
            pltpu.VMEM((D, D), BF),
            pltpu.VMEM((ROWS, D), BF),
            pltpu.SemaphoreType.DMA((1,)),
        ],
    )(meta, x2, dn2, og, vp, mixed, own, *arrays)


def attention_back_kernel(q, k, v, do, lse_ref, cos, sin, pq, pk, pv, dk, dv):
    masks = tile_masks()

    def one_pair(p, carry):
        lanes = pl.ds(pl.multiple_of(p * PAIR, PAIR), PAIR)
        dk[...] = jnp.zeros_like(dk)
        dv[...] = jnp.zeros_like(dv)
        for noised in (True, False):
            for t in range(SEQ // TILE):
                row = (0 if noised else SEQ) + TILE * t
                qs = head_split(q[pl.ds(row, TILE), lanes])
                ds = head_split(do[pl.ds(row, TILE), lanes])
                lse = jnp.concatenate(
                    [lse_ref[p, 0:1, row : row + TILE], lse_ref[p, 1:2, row : row + TILE]], axis=1
                )
                parts = key_parts(noised, t, masks)
                probs = [jnp.exp(s - lse) for s in masked_scores(k, lanes, parts, qs)]
                prods = []
                for (start, count, _), e in zip(parts, probs):
                    prods.append(e * mm(v[pl.ds(start, count), lanes], ds, NT))
                    dv[start : start + count, :] += mm(e.astype(BF), ds)
                dot = total_of([jnp.sum(x, axis=0, keepdims=True) for x in prods])
                dq = None
                for (start, count, _), e, x in zip(parts, probs, prods):
                    g = (x - e * dot).astype(BF)
                    dk[start : start + count, :] += mm(g, qs)
                    one = mm(k[pl.ds(start, count), lanes], g, TN)
                    dq = one if dq is None else dq + one
                dq = head_join(dq).T * 0.125
                at = TILE * t
                turn = dq * cos[at : at + TILE, :] - half_swap(dq) * sin[at : at + TILE, :]
                pq[pl.ds(row, TILE), lanes] = turn.astype(BF)
        for half in range(2):
            rows = slice(half * SEQ, (half + 1) * SEQ)
            z = dk[rows, :]
            pk[rows, lanes] = (z * cos[...] - half_swap(z) * sin[...]).astype(BF)
            pv[rows, lanes] = dv[rows, :].astype(BF)
        return carry

    lax.fori_loop(0, NPAIR, one_pair, 0)


def run_attention_back(q, k, v, do, lse, cos, sin):
    vm = pl.BlockSpec(memory_space=pltpu.VMEM)
    sq = jax.ShapeDtypeStruct((ROWS, D), BF)
    return pl.pallas_call(
        attention_back_kernel,
        name="attention_back",
        out_shape=(sq, sq, sq),
        in_specs=[vm] * 7,
        out_specs=(vm,) * 3,
        scratch_shapes=[pltpu.VMEM((ROWS, PAIR), F32), pltpu.VMEM((ROWS, PAIR), F32)],
    )(q, k, v, do, lse, cos, sin)


def qkv_grad_kernel(plans, nwide, meta, n1, pq, pk, pv, gwo, *refs):
    outs = (refs[0:2], refs[2:4])
    res, sems = refs[4:]
    start_scatter(gwo, *outs[1], 1, plans[1], nwide, meta, sems.at[3])
    for i, x in enumerate((pq, pk, pv)):
        res[i] = mm(x[...], n1[...], TN).astype(BF)
        start_scatter(
            res.at[i], *outs[i // 2], i % 2, plans[i // 2], nwide, meta, sems.at[i]
        )
    for i in range(3):
        wait_block(res.at[i], sems.at[i])
    wait_block(gwo, sems.at[3])


def run_qkv_grad(meta, n1, pq, pk, pv, gwo, plans, nwide):
    vm = pl.BlockSpec(memory_space=pltpu.VMEM)
    return pl.pallas_call(
        partial(qkv_grad_kernel, plans, nwide),
        name="qkv_grad",
        out_shape=(scatter_shape(nwide, 2),) * 4,
        in_specs=[pl.BlockSpec(memory_space=pltpu.SMEM)] + [vm] * 5,
        out_specs=(any_spec(),) * 4,
        scratch_shapes=[pltpu.VMEM((3, D, D), BF), pltpu.SemaphoreType.DMA((4,))],
    )(meta, n1, pq, pk, pv, gwo)


def input_grad_kernel(shapes, meta, tok, maskc, vp, dx2, pq, pk, pv, own, *refs):
    nw = sum(n for n, _ in shapes)
    first = split_refs(shapes, refs)
    in_ref, ge_ref, gg_ref = refs[nw : nw + 3]
    wbuf, sems = refs[nw + 3 :]
    start_blocks(meta, 3, own, first, wbuf, sems)
    for b in range(3):
        wait_block(wbuf.at[b], sems.at[b])
    gg = jnp.zeros((1, D), F32)
    kept = None
    for half in range(2):
        rows = slice(half * SEQ, (half + 1) * SEQ)
        dn = total_of([mm(x[rows, :], wbuf[b], NT) for b, x in enumerate((pq, pk, pv))])
        cen, r = norm_stats(input_rows(tok, maskc, vp, half))
        zh = cen * r
        gg = gg + jnp.sum(dn * zh, axis=0, keepdims=True)
        dx = dx2[rows, :] + norm_back(zh, r, dn * vp[1:2, :])
        if half == 0:
            hit = maskc[...] == 1
            ge_ref[...] = jnp.sum(jnp.where(hit, dx, 0.0), axis=0, keepdims=True)
            kept = jnp.where(hit, 0.0, dx)
        else:
            in_ref[...] = (dx + kept).astype(BF)
    gg_ref[...] = gg


def run_input_grad(meta, tok, maskc, vp, dx2, pq, pk, pv, own, first):
    vm = pl.BlockSpec(memory_space=pltpu.VMEM)
    arrays = group_arrays(first)
    return pl.pallas_call(
        partial(input_grad_kernel, group_shapes(first)),
        name="input_grad",
        out_shape=(
            jax.ShapeDtypeStruct((SEQ, D), BF),
            jax.ShapeDtypeStruct((1, D), F32),
            jax.ShapeDtypeStruct((1, D), F32),
        ),
        in_specs=[pl.BlockSpec(memory_space=pltpu.SMEM)] + [vm] * 7 + [any_spec()] * (1 + len(arrays)),
        out_specs=(vm,) * 3,
        scratch_shapes=[pltpu.VMEM((3, D, D), BF), pltpu.SemaphoreType.DMA((3,))],
    )(meta, tok, maskc, vp, dx2, pq, pk, pv, own, *arrays)


def send_kernel(scalars, direct, tree, *outs):
    outs[0][...] = direct[...].astype(BF)
    if len(outs) > 1:
        outs[1][...] = tree[...].astype(BF)


def run_send(scalars, weights, nwide, at, count, tree_at, tree_count):
    rows = D // nwide
    outs = [jax.ShapeDtypeStruct((count, D // 2, D), BF)]
    specs = [pl.BlockSpec((1, D // 2, D), lambda s, sc: (s, 0, 0))]
    if tree_count:
        outs.append(jax.ShapeDtypeStruct((tree_count, rows, D), BF))
        specs.append(
            pl.BlockSpec((1, rows, D), lambda s, sc: (jnp.minimum(s, tree_count - 1), 0, 0))
        )
    return pl.pallas_call(
        send_kernel,
        name="send_weights",
        grid_spec=pltpu.PrefetchScalarGridSpec(
            num_scalar_prefetch=1,
            grid=(count,),
            in_specs=[
                pl.BlockSpec((1, D // 2, D), lambda s, sc: (sc[2 + at + s], sc[1], 0)),
                pl.BlockSpec(
                    (1, rows, D),
                    lambda s, sc: (sc[2 + tree_at + jnp.minimum(s, max(tree_count, 1) - 1)], sc[0], 0),
                ),
            ],
            out_specs=tuple(specs),
        ),
        out_shape=tuple(outs),
    )(scalars, weights, weights)


def turn_kernel(count, sizes, shapes, meta, items, slots, *refs):
    grads = refs[: len(sizes)]
    refs = refs[len(sizes) :]
    nw = sum(n for n, _ in shapes)
    (left,) = split_refs(shapes, refs)
    out = refs[nw]
    lbuf, gbuf, lsem, gsem = refs[nw + 1 :]

    def begin(s, carry):
        item = items[s]
        at = 0
        for ref, size in zip(grads, sizes):

            @pl.when((item >= at) & (item < at + size))
            def _(ref=ref, at=at):
                pltpu.make_async_copy(ref.at[item - at], gbuf.at[s], gsem.at[s]).start()

            at += size
        start_slices(left, slots[s], lbuf.at[s], lsem.at[s], meta[0])
        return carry

    lax.fori_loop(0, count, begin, 0)
    parts = []
    for s in range(count):
        wait_block(gbuf.at[s], gsem.at[s])
        wait_block(lbuf.at[s], lsem.at[s])
        parts.append(mm(lbuf[s], gbuf[s], NT))
    out[...] = jnp.concatenate(parts, axis=1).astype(BF)


def run_turn(meta, items, slots, grads, left):
    count = items.shape[0]
    rows = grads[0].shape[1]
    sizes = tuple(g.shape[0] for g in grads)
    smem = pl.BlockSpec(memory_space=pltpu.SMEM)
    return pl.pallas_call(
        partial(turn_kernel, count, sizes, group_shapes([left])),
        name="gradient_turn",
        out_shape=jax.ShapeDtypeStruct((D, count * rows), BF),
        in_specs=[smem] * 3 + [any_spec()] * (len(grads) + len(left.arrays)),
        out_specs=pl.BlockSpec(memory_space=pltpu.VMEM),
        scratch_shapes=[
            pltpu.VMEM((count, D, D), BF),
            pltpu.VMEM((count, rows, D), BF),
            pltpu.SemaphoreType.DMA((count,)),
            pltpu.SemaphoreType.DMA((count,)),
        ],
    )(meta, items, slots, *grads, *left.arrays)


def adam_kernel(count, chained, slots, live, grads, first, second, right, *refs):
    nf, ns, back, full = refs[2 if chained else 0 :]
    s = pl.program_id(0)
    rows = first.shape[1]

    @pl.when(s == 0)
    def _():
        for k in range(count):
            for src in range(D // rows):
                at = slice(src * rows, (src + 1) * rows)
                full[k, :, at] = grads[at, k * rows : (k + 1) * rows].astype(F32)

    @pl.when(live[s] == 1)
    def _():
        basis = right[0].astype(BF)
        turned = mm(full[s].astype(BF), basis)
        one = BETA * first[0] + (1.0 - BETA) * turned
        two = BETA * second[0] + (1.0 - BETA) * turned * turned
        nf[0] = one
        ns[0] = two
        step = one / (jnp.sqrt(two) + EPS_ADAM)
        back[0] = mm(step.astype(BF), basis, NT).astype(BF)

    @pl.when(live[s] == 0)
    def _():
        nf[...] = jnp.zeros_like(nf)
        ns[...] = jnp.zeros_like(ns)
        back[...] = jnp.zeros_like(back)


def run_adam(slots, live, grads, first, second, right, earlier):
    count = slots.shape[0]
    rows = first.shape[1]
    state = pl.BlockSpec((1, rows, D), lambda s, slots, live: (slots[s], 0, 0))
    return pl.pallas_call(
        partial(adam_kernel, count, bool(earlier)),
        name="adam_step",
        grid_spec=pltpu.PrefetchScalarGridSpec(
            num_scalar_prefetch=2,
            grid=(count,),
            in_specs=[
                pl.BlockSpec(grads.shape, lambda s, *_: (0, 0)),
                state,
                state,
                pl.BlockSpec((1, D, D), lambda s, slots, live: (slots[s], 0, 0)),
            ]
            + [any_spec()] * len(earlier),
            out_specs=(state, state, pl.BlockSpec((1, rows, D), lambda s, *_: (s, 0, 0))),
            scratch_shapes=[pltpu.VMEM((count, rows, D), F32)],
        ),
        out_shape=(
            jax.ShapeDtypeStruct(first.shape, F32),
            jax.ShapeDtypeStruct(first.shape, F32),
            jax.ShapeDtypeStruct((count, rows, D), BF),
        ),
        input_output_aliases={6: 0, 7: 1} if earlier else {},
    )(slots, live, grads, first, second, right, *earlier)


def update_kernel(shapes, half, chained, slots, live, meta, weights, *refs):
    nw = sum(n for n, _ in shapes)
    back_a, back_b, left = split_refs(shapes, refs)
    out, lbuf, bbuf, lsem, bsem = refs[nw + (1 if chained else 0) :]
    s = pl.program_id(0)
    count = pl.num_programs(0)
    me = meta[0]
    slot = s % 2

    def begin(item, where):
        @pl.when(live[item] == 1)
        def _():
            @pl.when(item < half)
            def _():
                start_slices(back_a, item, bbuf.at[where], bsem.at[where], me)

            @pl.when(item >= half)
            def _():
                start_slices(back_b, item - half, bbuf.at[where], bsem.at[where], me)

            start_slices(left, slots[item], lbuf.at[where], lsem.at[where], me)

    @pl.when(s == 0)
    def _():
        begin(0, 0)

    @pl.when(s + 1 < count)
    def _():
        begin(s + 1, 1 - slot)

    @pl.when(live[s] == 1)
    def _():
        wait_block(lbuf.at[slot], lsem.at[slot])
        wait_block(bbuf.at[slot], bsem.at[slot])
        out[0] = weights[0] - RATE_MATRIX * mm(lbuf[slot], bbuf[slot], TN)

    @pl.when(live[s] == 0)
    def _():
        out[...] = jnp.zeros_like(out)


def run_update(slots, live, meta, weights, backs, half, left, earlier):
    groups = backs + [left]
    arrays = group_arrays(groups)
    whole = pl.BlockSpec((1, D, D), lambda s, slots, *_: (slots[s], 0, 0))
    return pl.pallas_call(
        partial(update_kernel, group_shapes(groups), half, bool(earlier)),
        name="weight_update",
        grid_spec=pltpu.PrefetchScalarGridSpec(
            num_scalar_prefetch=3,
            grid=(slots.shape[0],),
            in_specs=[whole] + [any_spec()] * (len(arrays) + len(earlier)),
            out_specs=whole,
            scratch_shapes=[
                pltpu.VMEM((2, D, D), BF),
                pltpu.VMEM((2, D, D), BF),
                pltpu.SemaphoreType.DMA((2,)),
                pltpu.SemaphoreType.DMA((2,)),
            ],
        ),
        out_shape=jax.ShapeDtypeStruct(weights.shape, F32),
        input_output_aliases={4 + len(arrays): 0} if earlier else {},
    )(slots, live, meta, weights, *arrays, *earlier)


def rotary_tables():
    half_size = D // HEADS // 2
    position_col = jnp.arange(SEQ, dtype=jnp.int32).astype(F32)
    frequency = jnp.exp(
        jnp.arange(half_size, dtype=F32) * (-2.0 * math.log(10000.0) / (2 * half_size))
    )
    angles = position_col[:, None] * frequency[None, :]
    cosine = jnp.cos(angles)
    sine = jnp.sin(angles)
    return (
        jnp.concatenate([cosine, cosine, cosine, cosine], axis=1),
        jnp.concatenate([-sine, sine, -sine, sine], axis=1),
    )


def on_device(nwide, nnarrow, *args):
    return whole_step(nwide, nnarrow, *args)


def whole_step(
    nwide,
    nnarrow,
    tokens,
    masked,
    out_grad,
    slot_block,
    weights,
    vectors,
    vec_first,
    vec_second,
    mom_first,
    mom_second,
    basis_left,
    basis_right,
):
    sd = weights.shape[0]
    slots = sd * nnarrow
    w = lax.axis_index("wide").astype(jnp.int32)
    n = lax.axis_index("narrow").astype(jnp.int32)
    top = nnarrow // 2
    nbit = n // top
    far_order = far_bits(nwide)
    left_order = far_order[:1] + far_order[-2:-1] + far_order[1:-2] + far_order[-1:]
    inner = [("wide", nwide, bit) for bit in far_order[-2::-1]]
    split = [("narrow", nnarrow, top)]
    near_x = tuple(split + inner)
    near_y = tuple(inner[:1] + split + inner[1:])

    ids = jnp.arange(slots, dtype=jnp.int32)
    hits = slot_block[None, :] == jnp.arange(NBLK, dtype=jnp.int32)[:, None]
    block_slot = jnp.sum(jnp.where(hits, ids[None, :], 0), axis=1)
    earlier = (
        (slot_block[None, :] < slot_block[:, None])
        | ((slot_block[None, :] == slot_block[:, None]) & (ids[None, :] < ids[:, None]))
    ) & (ids[None, :] // sd == ids[:, None] // sd)
    slot_rank = jnp.sum(earlier.astype(jnp.int32), axis=1)
    block_rank = jnp.sum(jnp.where(hits, slot_rank[None, :], 0), axis=1)
    own_blocks = lax.dynamic_slice_in_dim(slot_block, n * sd, sd)
    own_rank = lax.dynamic_slice_in_dim(slot_rank, n * sd, sd)
    at_rank = own_rank[None, :] == jnp.arange(sd, dtype=jnp.int32)[:, None]
    sorted_slots = jnp.sum(
        jnp.where(at_rank, jnp.arange(sd, dtype=jnp.int32)[None, :], 0), axis=1
    )
    sorted_blocks = jnp.sum(jnp.where(at_rank, own_blocks[None, :], 0), axis=1)
    sorted_live = (sorted_blocks < NBLK).astype(jnp.int32)

    scalars = jnp.concatenate([w[None], (w & 1)[None], sorted_slots]).astype(jnp.int32)
    c1 = min(4, sd)
    d1 = c1 // 2
    pieces = [("d1", 0, d1, True), ("t1", d1, c1 - d1, False)]
    if sd > c1:
        mid = (sd - c1) // 2
        pieces += [("d2", c1, mid, True), ("t2", c1 + mid, sd - c1 - mid, False)]

    def spread(x, direct):
        got = narrow_parts(x, nnarrow)[1:]
        got = got[0] if len(got) == 1 else jnp.concatenate(got, axis=0)
        if direct:
            return wide_group(got, nwide, [1], 0)
        return wide_group(got, nwide, far_order, len(far_order) - 2)

    direct, tree = run_send(scalars, weights, nwide, 0, d1, d1, c1 - d1)
    early_tree = spread(tree, False)
    early_direct = spread(direct, True)
    first = [early_direct, early_tree]
    groups = list(first)
    if sd > c1:
        direct, tree = run_send(scalars, weights, nwide, c1, mid, c1 + mid, sd - c1 - mid)
        groups += [spread(direct, True), spread(tree, False)]
    own = weights.astype(BF)

    far = n ^ (block_slot // sd)
    source = jnp.zeros((NBLK,), jnp.int32)
    index = block_slot % sd
    for k, (_, at, count, _) in enumerate(pieces):
        here = (far > 0) & (block_rank >= at) & (block_rank < at + count)
        source = jnp.where(here, k + 1, source)
        index = jnp.where(here, (far - 1) * count + block_rank - at, index)
    meta = jnp.concatenate([w[None], nbit[None], source, index]).astype(jnp.int32)

    vec_rel = jnp.stack(narrow_parts(vectors.astype(BF), nnarrow))
    vec_all = vec_rel[n ^ jnp.arange(nnarrow, dtype=jnp.int32)].reshape(8, D).astype(F32)

    left = basis_left.transpose(0, 2, 1).astype(BF)
    left = wide_group(left, nwide, left_order, len(left_order) - 2)

    cos, sin = rotary_tables()
    tok = tokens[0]
    maskc = masked[0][:, None]
    og = out_grad[0]

    q, k, v, n1 = run_qkv(meta, tok, maskc, vec_all, cos, sin, own, first)
    mixed, lse, x2, n2 = run_forward(meta, tok, maskc, vec_all, q, k, v, own, first)
    layer_out, up_keep, up_send, down_keep, down_send, dn2, gbias = run_ffn(
        meta, n2, og, x2, vec_all, own, groups, (near_y, near_x), nwide
    )

    def reduced(keep, send, steps):
        total = scatter_sum(keep, send, nwide, steps)
        rest = far_bits(nnarrow)[1:]
        total = butterfly_sum(total, "narrow", nnarrow, rest, BF).astype(BF)
        return [total, xor_permute(total, "narrow", nnarrow, top)]

    gdown = reduced(down_keep, down_send, near_x)
    gup = reduced(up_keep, up_send, near_y)
    dx2, do, gwo, gg2 = run_resid(meta, x2, dn2, og, vec_all, mixed, own, first)
    pq, pk, pv = run_attention_back(q, k, v, do, lse, cos, sin)
    qk_keep, qk_send, vo_keep, vo_send = run_qkv_grad(
        meta, n1, pq, pk, pv, gwo, (near_x, near_y), nwide
    )
    gqk = reduced(qk_keep, qk_send, near_x)
    gvo = reduced(vo_keep, vo_send, near_y)
    in_grad, ge, gg1 = run_input_grad(
        meta, tok, maskc, vec_all, dx2, pq, pk, pv, own, first
    )

    chunks = [(0, c1, 0)]
    if sd > c1:
        chunks = [(c1, sd, 4)] + chunks
    state = ()
    fresh = ()
    ffn_grads = jnp.concatenate(gup + gdown, axis=0)
    att_grads = jnp.concatenate(gqk + gvo, axis=0)
    for lo, hi, base in chunks:
        grads = [ffn_grads] if base else [att_grads, ffn_grads]
        block = jnp.clip(sorted_blocks[lo:hi], base, NBLK - 1)
        width = jnp.where(block < 4, 1, 2)
        start = jnp.where(block < 4, block // 2 * 2, block // 4 * 4)
        items = start - base + ((block & 1) ^ nbit) * width + (block - start) // 2
        held = sorted_slots[lo:hi]
        live = sorted_live[lo:hi]
        turned = run_turn(meta, items, held, grads, left)
        turned = lax.all_to_all(turned, "wide", 0, 0, tiled=True)
        *state, back = run_adam(
            held, live, turned, mom_first, mom_second, basis_right, state
        )
        half = (hi - lo + 1) // 2
        merge = len(far_order) - 2
        backs = [
            wide_group(back[:half], nwide, far_order, merge),
            wide_group(back[half:], nwide, left_order, merge),
        ]
        fresh = (run_update(held, live, meta, weights, backs, half, left, fresh),)
    new_first, new_second = state
    new_weights = fresh[0]

    vec_grad = jnp.concatenate([ge, gg1, gg2, gbias[: FFB + 1]], axis=0)
    vec_grad = butterfly_sum(vec_grad, "narrow", nnarrow, far_bits(nnarrow))
    for bit in far_order[:-1]:
        vec_grad = butterfly_sum(vec_grad, "wide", nwide, [bit])
    vec_grad = butterfly_sum(vec_grad, "wide", nwide, far_order[-1:])
    vec_owned = lax.dynamic_slice_in_dim(
        vec_grad.reshape(nnarrow, vectors.shape[0]), n, 1, axis=0
    )[0]
    vec_mean = BETA * vec_first + (1.0 - BETA) * vec_owned
    vec_square = BETA * vec_second + (1.0 - BETA) * vec_owned * vec_owned
    vec_new = vectors - RATE_VECTOR * vec_mean / (jnp.sqrt(vec_square) + EPS_ADAM)
    return (
        layer_out[None],
        in_grad[None],
        new_weights,
        new_first,
        new_second,
        vec_new,
        vec_mean,
        vec_square,
    )


def solution(mesh):
    return jax.shard_map(
        partial(on_device, mesh.shape["wide"], mesh.shape["narrow"]),
        mesh=mesh,
        in_specs=(
            P(("wide", "narrow"), None, None),
            P(("wide", "narrow"), None),
            P(("wide", "narrow"), None, None),
            P(),
            P("narrow", None, None),
            P("narrow"),
            P("narrow"),
            P("narrow"),
            P("narrow", "wide", None),
            P("narrow", "wide", None),
            P("narrow", None, "wide"),
            P("narrow", None, None),
        ),
        out_specs=(
            P(("wide", "narrow"), None, None),
            P(("wide", "narrow"), None, None),
            P("narrow", None, None),
            P("narrow", "wide", None),
            P("narrow", "wide", None),
            P("narrow"),
            P("narrow"),
            P("narrow"),
        ),
        check_vma=False,
    )
```
